128 devices in a mesh: dp: 4 (over z), expert: 32 (over x, y, core).
Axes of the slice: x: 4, y: 4, z: 4, core: 2. Of those that a mesh axis runs over, the one named last changes fastest.
Arguments:
- tokens: bfloat16 [4096, 4096], P(('dp', 'expert')), may hold values from -6 to 6
- cotangent: bfloat16 [4096, 4096], P(('dp', 'expert')), may hold values from -6 to 6
- start: bfloat16 [4096, 4096], P(('dp', 'expert')), may hold values from -64 to 64
- gates: float32 [4096, 8], P(('dp', 'expert')), may hold values from 0.05 to 0.45
- routes: int32 [4096, 8], P(('dp', 'expert')), may hold values from 0 to 127, all different within a row; in each aligned block of 32 rows (0 to 31, 32 to 63, ...) at most 3 rows name the same one
- w_gate: bfloat16 [128, 4096, 768], P(('dp', 'expert')), may hold values from -0.09375 to 0.09375
- w_up: bfloat16 [128, 4096, 768], P(('dp', 'expert')), may hold values from -1 to 1
- w_down: bfloat16 [128, 768, 4096], P(('dp', 'expert')), may hold values from -2 to 2
Outputs:
- basis: bfloat16 [4096, 4096], P(('dp', 'expert'))
- residual: float32 [4096, 4096], P(('dp', 'expert'))
- tridiagonal: float32 [4], replicated
The draws below stay inside these ranges and needn't reach their ends.
Inputs may be any that keep to these rules, and one draw needn't show every extreme that they name: `routes`: each token names 8 different experts; among the 32 tokens of one device (aligned blocks) no expert is named more than 3 times, a bound that some block reaches.
All inputs are finite; a program needn't handle non-finite values.
Results may differ from the reference program's by a relative error of at most 0.0074.
Values may be sent and summed in bfloat16 or wider, within the bound.
A program may use at most 128 MiB of HBM per device.

```python
import math
import jax
import jax.numpy as jnp
import numpy as np
from jax import lax

D = 4096
FF = 768
TOP = 8
TOK_DEV = 32
EXPERTS = 128
TOKENS = 4096
MOST = 3
N_DP = 4
N_EXPERT = 32


def draw_start(key, part):
    key_base, key_rows, key_cols = jax.random.split(jax.random.fold_in(key, 11), 3)
    position = jnp.arange(TOKENS, dtype=jnp.float32) / TOKENS
    row_scale = jnp.exp(jnp.log(10.0) * (0.5 * position + 0.5 * jax.random.uniform(key_rows, (TOKENS,), jnp.float32)))
    col_scale = jnp.exp(jnp.log(10.0) * jax.random.uniform(key_cols, (D,), jnp.float32))
    noise_base = jax.random.normal(key_base, (TOKENS, D), jnp.float32)
    values = noise_base * row_scale[:, None] * col_scale[None, :] / 10.0
    return jnp.clip(values, -64.0, 64.0).astype(jnp.bfloat16)


def unit_noise(key, shape):
    return jnp.clip(jax.random.normal(key, shape, jnp.float32), -6.0, 6.0)


def token_field(key):
    return unit_noise(jax.random.fold_in(key, 21), (TOKENS, D))


def up_field(key):
    return unit_noise(jax.random.fold_in(key, 31), (EXPERTS, D, FF)) * (1.0 / math.sqrt(D))


def draw_tokens(key, part):
    return token_field(key).astype(jnp.bfloat16)


def draw_cotangent(key, part):
    inputs = token_field(key)
    noise = unit_noise(jax.random.fold_in(key, 22), (TOKENS, D))
    position = jnp.arange(TOKENS, dtype=jnp.float32) / TOKENS
    share = 0.3 + 0.6 * position
    values = share[:, None] * inputs + jnp.sqrt(1.0 - share * share)[:, None] * noise
    return jnp.clip(values, -6.0, 6.0).astype(jnp.bfloat16)


def draw_w_up(key, part):
    return up_field(key).astype(jnp.bfloat16)


def draw_w_down(key, part):
    tied = jnp.swapaxes(up_field(key), 1, 2) * (0.8 * math.sqrt(D / FF))
    noise = unit_noise(jax.random.fold_in(key, 32), (EXPERTS, FF, D)) * (0.6 / math.sqrt(FF))
    return jnp.clip(tied + noise, -2.0, 2.0).astype(jnp.bfloat16)


def levels(rng, dims, pieces, smallest, largest):
    gain = 1.0
    for dim, parts in pieces:
        heights = jax.random.uniform(jax.random.fold_in(jax.random.fold_in(rng, 6), dim), (parts,), jnp.float32, smallest / len(pieces), largest / len(pieces))
        gain = gain * jnp.repeat(jnp.exp(heights), dims[dim] // parts).reshape((-1,) + (1,) * (len(dims) - 1 - dim))
    return gain


def assign_block(stream_key, own, number, rows, number_of, top, most, lean):
    sequence = jax.random.permutation(stream_key, number_of)
    heavy_load, common = load_shares(number_of, rows * top, most, lean, True), load_shares(number_of, rows * top, most, lean, False)
    places = jnp.arange(number_of)

    def named(lengths, offset_by):
        used = int((lengths > 0).sum())
        fixed = max(1, used // 4)
        shifted = fixed + (places - fixed + offset_by * (used - fixed)) % max(1, number_of - fixed)
        return jnp.zeros((number_of,), jnp.int32).at[sequence[jnp.where(places < fixed, places, shifted)]].set(jnp.asarray(lengths, jnp.int32))

    lengths = jnp.where(number % 4 == 0, named(heavy_load, number // 4), named(common, number - number // 4 - 1))
    mixed = jax.random.permutation(jax.random.fold_in(own, 3), number_of)
    source_of, sink = mixed[0:number_of // 2 * 2:2], mixed[1:number_of // 2 * 2:2]
    margin = jnp.minimum(lengths[source_of] - 1, most - lengths[sink]) // 2
    margin = jnp.where((source_of == sequence[0]) | (sink == sequence[0]) | (lengths[sink] == 0), 0, jnp.maximum(margin, 0))
    shifted = jax.random.randint(jax.random.fold_in(own, 4), (number_of // 2,), 0, 1 << 20) % (margin + 1)
    lengths = lengths.at[source_of].add(-shifted).at[sink].add(shifted)
    labels = jnp.searchsorted(jnp.cumsum(lengths), jnp.arange(rows * top), side="right").astype(jnp.int32)
    grid = labels.reshape(top, rows).T
    grid = grid[jax.random.permutation(jax.random.fold_in(own, 1), rows)]
    offset_by = jax.random.randint(jax.random.fold_in(own, 2), (rows, 1), 0, top)
    return jnp.take_along_axis(grid, (jnp.arange(top)[None, :] + offset_by) % top, axis=1)


def load_shares(amount, total, most, lean, full):
    weights = [(1 << 20) // math.isqrt(standing ** lean) + 1 for standing in range(1, amount + 1)]
    largest = most if full else min(most, max(-(-total // amount), total * weights[0] // sum(weights)))
    least = 1 if total - largest >= amount - 1 else 0
    given, spare = [largest] + [least] * (amount - 1), total - largest - least * (amount - 1)
    while spare > 0:
        movable = [i for i in range(1, amount) if given[i] < largest] or [i for i in range(1, amount) if given[i] < most]
        pool, remaining = sum([weights[i] for i in movable]), spare
        for i in movable:
            more = min(most - given[i], max(1, remaining * weights[i] // pool), spare)
            given[i] = given[i] + more
            spare = spare - more
    return np.array(given)


def bell_draw(key, extent, spread, most, shards=(), kind=jnp.bfloat16):
    values = jax.random.normal(key, extent, jnp.float32) * spread
    if len(shards) > 0:
        values = levels(key, extent, shards, -0.22, 0.18) * values
    return jnp.clip(values, min=-most, max=most).astype(kind)


def setup_inputs(seed: int = 0) -> dict:
    arg_keys = jax.random.split(jax.random.key(seed), 9)
    tokens = draw_tokens(jax.random.fold_in(arg_keys[8], 71), 0)
    cotangent = draw_cotangent(jax.random.fold_in(arg_keys[8], 71), 0)
    start = draw_start(jax.random.fold_in(arg_keys[8], 71), 0)
    gates = jnp.clip(0.05 + 0.39999999 * jax.random.uniform(arg_keys[3], (TOKENS, TOP), jnp.float32) ** levels(arg_keys[3], (TOKENS, TOP), ((0, 128),), -0.2, 0.2), 0.05, 0.45)
    routes_keys = jax.random.split(jax.random.fold_in(arg_keys[4], 1), TOKENS // TOK_DEV)
    routes_turns = jax.random.permutation(jax.random.fold_in(arg_keys[4], 3), TOKENS // TOK_DEV)
    routes = jax.vmap(lambda own, number: assign_block(jax.random.fold_in(arg_keys[4], 2), own, number, TOK_DEV, EXPERTS, TOP, MOST, 2))(routes_keys, routes_turns).reshape((TOKENS, TOP))
    w_gate = bell_draw(arg_keys[5], (EXPERTS, D, FF), D ** -0.5, 0.09375, ((0, 128),))
    w_up = draw_w_up(jax.random.fold_in(arg_keys[8], 71), 0)
    w_down = draw_w_down(jax.random.fold_in(arg_keys[8], 71), 0)
    return {"tokens": tokens, "cotangent": cotangent, "start": start, "gates": gates, "routes": routes, "w_gate": w_gate, "w_up": w_up, "w_down": w_down}


EPSILON = 1e-06

def silu_slopes(pre_gate):
    logistic = jax.nn.sigmoid(pre_gate)
    slope_one = logistic * (1.0 + pre_gate * (1.0 - logistic))
    slope_two = logistic * (1.0 - logistic) * (2.0 + pre_gate * (1.0 - 2.0 * logistic))
    return (slope_one, slope_two)

def reference(tokens, cotangent, start, gates, routes, w_gate, w_up, w_down):
    block_count = N_DP * N_EXPERT
    pair_count = TOK_DEV * TOP
    capacity = block_count * MOST
    flat_ids = routes.reshape(block_count, pair_count)
    columns = jnp.arange(EXPERTS, dtype=jnp.int32)
    onehot = (flat_ids[:, :, None] == columns[None, None, :]).astype(jnp.int32)
    before = jnp.cumsum(onehot, axis=1) - onehot
    rank = lax.optimization_barrier(jnp.sum(before * onehot, axis=2)).astype(jnp.int32)
    block_index = jnp.arange(block_count, dtype=jnp.int32)[:, None]
    slot = ((flat_ids * block_count + block_index) * MOST + rank).reshape(-1)
    pair_token = (block_index * TOK_DEV + jnp.arange(pair_count, dtype=jnp.int32)[None, :] // TOP).reshape(-1)
    slot_token = jnp.zeros((EXPERTS * capacity,), jnp.int32).at[slot].set(pair_token).reshape(EXPERTS, capacity)
    filled = jnp.zeros((EXPERTS * capacity,), jnp.float32).at[slot].set(1.0).reshape(EXPERTS, capacity)
    slot_gate = jnp.zeros((EXPERTS * capacity,), jnp.float32).at[slot].set(gates.reshape(-1)).reshape(EXPERTS, capacity)

    def prepare(inputs):
        token_index, keep_row, gate_row, gate_w, up_w, down_w = inputs
        keep = keep_row > 0.5
        x_rows = jnp.where(keep[:, None], tokens[token_index], jnp.zeros((), tokens.dtype))
        c_rows = (cotangent[token_index].astype(jnp.float32) * (gate_row * keep_row)[:, None]).astype(jnp.bfloat16)
        pre_gate = jnp.dot(x_rows, gate_w, preferred_element_type=jnp.float32)
        pre_up = jnp.dot(x_rows, up_w, preferred_element_type=jnp.float32)
        back_grad = jnp.dot(c_rows, down_w.T, preferred_element_type=jnp.float32)
        slope_one, slope_two = silu_slopes(pre_gate)
        return (back_grad * slope_one, back_grad * pre_up * slope_two)
    scale_one, scale_two = lax.map(prepare, (slot_token, filled, slot_gate, w_gate, w_up, w_down))

    def hessian_product(vector):

        def add_expert(total, inputs):
            token_index, keep_row, first_scale, second_scale, gate_w, up_w = inputs
            keep = keep_row > 0.5
            v_rows = jnp.where(keep[:, None], vector[token_index], jnp.zeros((), vector.dtype))
            along_gate = jnp.dot(v_rows, gate_w, preferred_element_type=jnp.float32)
            along_up = jnp.dot(v_rows, up_w, preferred_element_type=jnp.float32)
            out_gate = (first_scale * along_up + second_scale * along_gate).astype(jnp.bfloat16)
            out_up = (first_scale * along_gate).astype(jnp.bfloat16)
            summed = jnp.dot(out_gate, gate_w.T, preferred_element_type=jnp.float32) + jnp.dot(out_up, up_w.T, preferred_element_type=jnp.float32)
            rounded = lax.optimization_barrier(summed.astype(jnp.bfloat16))
            return (total.at[token_index].add(rounded.astype(jnp.float32)), None)
        initial = jnp.zeros((TOKENS, D), jnp.float32)
        total, _ = lax.scan(add_expert, initial, (slot_token, filled, scale_one, scale_two, w_gate, w_up))
        return total
    entry_total = float(TOKENS * D)
    anchor = start.astype(jnp.float32)
    anchor_norm = jnp.sqrt(jnp.sum(anchor * anchor) / entry_total + EPSILON)
    base = anchor / anchor_norm
    image_zero = hessian_product(start)
    alpha_zero = jnp.sum(anchor * image_zero) / entry_total / (anchor_norm * anchor_norm)
    first_resid = image_zero / anchor_norm - alpha_zero * base
    beta_one = jnp.sqrt(jnp.sum(first_resid * first_resid) / entry_total + EPSILON)
    basis = (first_resid / beta_one).astype(jnp.bfloat16)
    image_one = hessian_product(basis)
    basis_wide = basis.astype(jnp.float32)
    alpha_one = jnp.sum(basis_wide * image_one) / entry_total
    residual = image_one - alpha_one * basis_wide - beta_one * base
    beta_two = jnp.sqrt(jnp.sum(residual * residual) / entry_total + EPSILON)
    return (basis, residual, jnp.stack([alpha_zero, beta_one, alpha_one, beta_two]))
```

```python
import functools
import jax
import jax.numpy as jnp
from jax import lax
from jax.experimental import pallas as pl
from jax.experimental.pallas import tpu as pltpu
from jax.sharding import PartitionSpec as P

EPSILON = 1e-06
MESH = pl.DeviceIdType.MESH
F32 = jnp.float32
BF16 = jnp.bfloat16
SUB = 16
ORDERS = (("z", "x", "y"), ("x", "y", "z"), ("y", "z", "x"))
ANY = pl.BlockSpec(memory_space=pl.ANY)
VM = pl.BlockSpec(memory_space=pltpu.VMEM)


def rem(value, size):
    return lax.rem(value, jnp.int32(size))


def here():
    expert = lax.axis_index("expert")
    return {
        "z": lax.axis_index("dp"),
        "x": expert // 8,
        "y": rem(expert // 2, 4),
        "c": rem(expert, 2),
    }


def device_of(place):
    return (place["z"], place["x"] * 8 + place["y"] * 2 + place["c"])


def offsets(axes):
    if len(axes) == 1:
        return [(0,), (1,), (3,), (2,)]
    return [(0, 0), (0, 1), (1, 0), (3, 0), (1, 1), (3, 1), (2, 0), (2, 1)]


def size_of(axes):
    return 4 if len(axes) == 1 else 8


def index_of(place, axes):
    value = place[axes[0]]
    return value * 2 + place["c"] if len(axes) == 2 else value


def moved(place, axes, step, sign=1):
    new = dict(place)
    for axis, amount in zip(axes, step):
        count = 2 if axis == "c" else 4
        new[axis] = rem(place[axis] + (amount if sign > 0 else count - amount), count)
    return new


def slot_id(axes, step):
    return step[0] * 2 + step[1] if len(axes) == 2 else step[0]


def groups_of(order, back):
    first, second, third = (order[0],), (order[1],), (order[2], "c")
    return (third, second, first) if back else (first, second, third)


def peers_of(place):
    found = []
    for axis in ("z", "x", "y"):
        for amount in (1, 2, 3):
            near = moved(place, (axis,), (amount,))
            found.append(near)
            found.append(moved(near, ("c",), (1,)))
    found.append(moved(place, ("c",), (1,)))
    return found


def entry_barrier(places):
    barrier = pltpu.get_barrier_semaphore()
    for place in places:
        pl.semaphore_signal(barrier, inc=1, device_id=device_of(place), device_id_type=MESH)
    pl.semaphore_wait(barrier, len(places))


REDUCE_GROUPS = (("z",), ("x",), ("y", "c"))


class Reduction:
    def __init__(self, place, tiles, send_sem, recv_sem):
        self.place, self.tiles = place, tiles
        self.send_sem, self.recv_sem = send_sem, recv_sem

    def send(self, level, value):
        axes, place = REDUCE_GROUPS[level], self.place
        tile = self.tiles[level]
        mine = index_of(place, axes)
        tile[mine] = value
        for step in offsets(axes)[1:]:
            pltpu.make_async_remote_copy(
                tile.at[mine],
                tile.at[mine],
                self.send_sem.at[level],
                self.recv_sem.at[level],
                device_id=device_of(moved(place, axes, step)),
                device_id_type=MESH,
            ).start()

    def receive(self, level):
        axes, place = REDUCE_GROUPS[level], self.place
        tile = self.tiles[level]
        count = size_of(axes)
        rest = tile.at[pl.ds(0, count - 1)]
        bulk = pltpu.make_async_remote_copy(
            rest,
            rest,
            self.send_sem.at[level],
            self.recv_sem.at[level],
            device_id=device_of(moved(place, axes, offsets(axes)[1])),
            device_id_type=MESH,
        )
        bulk.wait_send()
        bulk.wait_recv()
        total = tile[0]
        for index in range(1, count):
            total = total + tile[index]
        return total


def reduction_scratch():
    return [
        pltpu.VMEM((4, 8, 128), F32),
        pltpu.VMEM((4, 8, 128), F32),
        pltpu.VMEM((8, 8, 128), F32),
        pltpu.SemaphoreType.DMA((3,)),
        pltpu.SemaphoreType.DMA((3,)),
    ]


def exchange_kernel(back, summing, *refs):
    blocks = refs[:3]
    refs = refs[3:]
    if summing:
        part, refs = refs[0], refs[1:]
    outs, refs = refs[:3], refs[3:]
    if summing:
        total, refs = refs[0], refs[1:]
    first_hold, second_hold, refs = refs[:3], refs[3:6], refs[6:]
    (send_one, send_two, send_three, recv_one, recv_two, recv_three, local_one, local_two, local_three) = refs[:9]
    place = here()
    plans = [groups_of(order, back) for order in ORDERS]
    if summing:
        tiles, (sum_send, sum_recv) = refs[9:12], refs[12:14]
        reduction = Reduction(place, tiles, sum_send, sum_recv)
    entry_barrier(peers_of(place))

    def remote(src, dst, send_sem, recv_sem, target):
        return pltpu.make_async_remote_copy(
            src, dst, send_sem, recv_sem, device_id=device_of(target), device_id_type=MESH
        )

    if summing:
        reduction.send(0, part[...])
    for turn in range(8):
        for r, (one, two, three) in enumerate(plans):
            if turn >= size_of(one):
                continue
            step = offsets(one)[turn]
            mine = index_of(place, one)
            if turn == 0:
                pltpu.make_async_copy(blocks[r].at[mine], first_hold[r].at[mine], local_one.at[r]).start()
                continue
            target = moved(place, one, step)
            remote(
                blocks[r].at[index_of(target, one)],
                first_hold[r].at[mine],
                send_one.at[r],
                recv_one.at[r, slot_id(one, step)],
                target,
            ).start()
    for turn in range(8):
        for r, (one, two, three) in enumerate(plans):
            if turn >= size_of(one):
                continue
            step = offsets(one)[turn]
            mine_one, mine_two = index_of(place, one), index_of(place, two)
            if turn == 0:
                source = mine_one
                pltpu.make_async_copy(blocks[r].at[source], first_hold[r].at[source], local_one.at[r]).wait()
            else:
                origin = moved(place, one, step, -1)
                source = index_of(origin, one)
                held = first_hold[r].at[source]
                remote(held, held, send_one.at[r], recv_one.at[r, slot_id(one, step)], origin).wait_recv()
            for hop in offsets(two)[1:]:
                target = moved(place, two, hop)
                remote(
                    first_hold[r].at[source, index_of(target, two)],
                    second_hold[r].at[mine_two, source],
                    send_two.at[r],
                    recv_two.at[r, slot_id(two, hop)],
                    target,
                ).start()
            pltpu.make_async_copy(
                first_hold[r].at[source, mine_two], second_hold[r].at[mine_two, source], local_two.at[r]
            ).start()
    if summing:
        reduction.send(1, reduction.receive(0))
    for turn in range(4):
        for r, (one, two, three) in enumerate(plans):
            step = offsets(two)[turn]
            mine_two, mine_three = index_of(place, two), index_of(place, three)
            if turn == 0:
                source = mine_two
                held = second_hold[r].at[source]
                pltpu.make_async_copy(held, held, local_two.at[r]).wait()
            else:
                origin = moved(place, two, step, -1)
                source = index_of(origin, two)
                held = second_hold[r].at[source]
                remote(held, held, send_two.at[r], recv_two.at[r, slot_id(two, step)], origin).wait_recv()
            for hop in offsets(three)[1:]:
                target = moved(place, three, hop)
                remote(
                    second_hold[r].at[source, :, index_of(target, three)],
                    outs[r].at[mine_three, source],
                    send_three.at[r],
                    recv_three.at[r],
                    target,
                ).start()
            pltpu.make_async_copy(
                second_hold[r].at[source, :, mine_three], outs[r].at[mine_three, source], local_three.at[r]
            ).start()
    if summing:
        reduction.send(2, reduction.receive(1))
        total[...] = reduction.receive(2)
    near = moved(place, ("c",), (1,))
    for r, (one, two, three) in enumerate(plans):
        rest = blocks[r].at[pl.ds(0, size_of(one) - 1)]
        remote(rest, rest, send_one.at[r], recv_three.at[r], near).wait_send()
        rest = second_hold[r].at[pl.ds(0, 3)]
        remote(rest, rest, send_two.at[r], recv_three.at[r], near).wait_send()
        rest = outs[r].at[pl.ds(0, size_of(three) - 1)]
        bulk = remote(rest, rest, send_three.at[r], recv_three.at[r], near)
        bulk.wait_send()
        bulk.wait_recv()
        mine = outs[r].at[index_of(place, three)]
        pltpu.make_async_copy(mine, mine, local_three.at[r]).wait()


def exchange(blocks, back, number, part=None):
    sub, lanes = blocks[0].shape[1:]
    dims_in = (8, 4, 4) if back else (4, 4, 8)
    dims_out = dims_in[::-1]
    one, two, three = dims_in
    summing = part is not None
    scratch = [pltpu.VMEM((one, two, three, sub, lanes), BF16)] * 3
    scratch += [pltpu.VMEM((two, one, three, sub, lanes), BF16)] * 3
    scratch += [pltpu.SemaphoreType.DMA((3,))] * 3
    scratch += [pltpu.SemaphoreType.DMA((3, 8))] * 2
    scratch += [pltpu.SemaphoreType.DMA((3,))] * 4
    out_shape = [jax.ShapeDtypeStruct(dims_out + (sub, lanes), BF16)] * 3
    operands = [block.reshape(dims_in + (sub, lanes)) for block in blocks]
    in_specs, out_specs = [ANY] * 3, [ANY] * 3
    if summing:
        operands.append(part)
        in_specs.append(VM)
        out_specs.append(VM)
        out_shape.append(jax.ShapeDtypeStruct((8, 128), F32))
        scratch += reduction_scratch()
    results = pl.pallas_call(
        functools.partial(exchange_kernel, back, summing),
        out_shape=out_shape,
        in_specs=in_specs,
        out_specs=out_specs,
        scratch_shapes=scratch,
        name="exchange_%d" % number,
        compiler_params=pltpu.CompilerParams(
            collective_id=number, has_side_effects=True, vmem_limit_bytes=48 << 20
        ),
    )(*operands)
    moved_blocks = [result.reshape(128, sub, lanes) for result in results[:3]]
    return (moved_blocks, results[3]) if summing else moved_blocks


def swap_matrix():
    row = lax.broadcasted_iota(jnp.int32, (256, 256), 0)
    column = lax.broadcasted_iota(jnp.int32, (256, 256), 1)
    hit = (row // 16 == rem(column, 16)) & (rem(row, 16) == column // 16)
    return hit.astype(F32).astype(BF16)


def pack(rows_ref, row_start, swap, out_ref, lane):
    def block(index, carry):
        start = pl.multiple_of(row_start + index * 16, 16)
        stacked = jnp.concatenate(
            [rows_ref[pl.ds(start, 16), j * 256 : (j + 1) * 256] for j in range(SUB)], axis=0
        )
        turned = jnp.dot(swap, stacked, preferred_element_type=F32).astype(BF16)
        out_ref[pl.ds(pl.multiple_of(index * 16, 16), 16), :, lane : lane + 256] = turned.reshape(16, 16, 256)
        return carry

    lax.fori_loop(0, 8, block, 0)


def unpack(in_ref, lane, swap, rows_ref, row_start):
    def block(index, carry):
        stacked = in_ref[pl.ds(pl.multiple_of(index * 16, 16), 16), :, lane : lane + 256].reshape(256, 256)
        turned = jnp.dot(swap, stacked, preferred_element_type=F32).astype(BF16)
        start = pl.multiple_of(row_start + index * 16, 16)
        for j in range(SUB):
            rows_ref[pl.ds(start, 16), j * 256 : (j + 1) * 256] = turned[j * 16 : (j + 1) * 16, :]
        return carry

    lax.fori_loop(0, 8, block, 0)


def expert_ids(order):
    position = lax.broadcasted_iota(jnp.int32, (128, 32), 0)
    value = {
        order[0]: position // 32,
        order[1]: rem(position // 8, 4),
        order[2]: rem(position // 2, 4),
    }
    return value["z"] * 32 + value["x"] * 8 + value["y"] * 2 + rem(position, 2)


def send_kernel(routes, gates, tokens, cotangent, start, out_a, out_b, out_c, pick_ref, rows):
    swap = swap_matrix()
    early = lax.broadcasted_iota(jnp.int32, (32, 32), 0) < lax.broadcasted_iota(jnp.int32, (32, 32), 1)
    early = early.astype(F32).astype(BF16)
    for r, out in enumerate((out_a, out_b, out_c)):
        ids = expert_ids(ORDERS[r])
        named = jnp.zeros((128, 32), F32)
        weight = jnp.zeros((128, 32), F32)
        for k in range(8):
            hit = routes[k : k + 1, :] == ids
            named = named + hit.astype(F32)
            weight = weight + jnp.where(hit, gates[k : k + 1, :], 0.0)
        before = jnp.dot(named.astype(BF16), early, preferred_element_type=F32)
        keep = (named > 0.5) & (before == float(r))
        pick = keep.astype(F32).astype(BF16)
        pick_ref[r] = pick
        slot_gate = jnp.sum(jnp.where(keep, weight, 0.0), axis=1, keepdims=True)
        for unit, source in enumerate((tokens, cotangent, start)):
            for part in range(4):
                columns = slice(part * 1024, (part + 1) * 1024)
                picked = jnp.dot(pick, source[:, columns], preferred_element_type=F32)
                if unit == 1:
                    picked = picked * slot_gate
                rows[:, columns] = picked.astype(BF16)
            pack(rows, 0, swap, out, unit * 256)


def send_messages(routes, gates, tokens, cotangent, start):
    message = jax.ShapeDtypeStruct((128, SUB, 768), BF16)
    return pl.pallas_call(
        send_kernel,
        out_shape=[message] * 3 + [jax.ShapeDtypeStruct((3, 128, 32), BF16)],
        in_specs=[VM] * 5,
        out_specs=[VM] * 4,
        scratch_shapes=[pltpu.VMEM((128, 4096), BF16)],
        name="send_messages",
        compiler_params=pltpu.CompilerParams(vmem_limit_bytes=32 << 20),
    )(routes.T, gates.T, tokens, cotangent, start)


CONTRACT_LAST = (((1,), (1,)), ((), ()))


def last_dot(left, right):
    return lax.dot_general(left, right, CONTRACT_LAST, preferred_element_type=F32)


def results_out(out_gate, out_up, gate_w, up_w, rows, swap, outs):
    def tile(index, carry):
        start = pl.multiple_of(index * 256, 256)
        summed = last_dot(out_gate[...], gate_w[pl.ds(start, 256), :])
        summed = summed + last_dot(out_up[...], up_w[pl.ds(start, 256), :])
        rows[:, pl.ds(start, 256)] = summed.astype(BF16)
        return carry

    lax.fori_loop(0, 16, tile, 0)
    for r in range(3):
        pack(rows, r * 128, swap, outs[r], 0)


def first_expert_kernel(
    in_a, in_b, in_c, gate_h, up_h, down_h, out_a, out_b, out_c, one_ref, two_ref, ag_ref, au_ref,
    gate_w, up_w, down_w, x_rows, c_rows, v_rows, out_gate, out_up, sems,
):
    copies = [
        pltpu.make_async_copy(src, dst, sems.at[i])
        for i, (src, dst) in enumerate(((gate_h, gate_w), (up_h, up_w), (down_h, down_w)))
    ]
    for copy in copies:
        copy.start()
    swap = swap_matrix()
    for r, source in enumerate((in_a, in_b, in_c)):
        for unit, rows in enumerate((x_rows, c_rows, v_rows)):
            unpack(source, unit * 256, swap, rows, r * 128)
    for copy in copies:
        copy.wait()

    def tile(index, carry):
        columns = pl.ds(pl.multiple_of(index * 256, 256), 256)
        gate_t, up_t = gate_w[:, columns], up_w[:, columns]
        pre_gate = jnp.dot(x_rows[...], gate_t, preferred_element_type=F32)
        pre_up = jnp.dot(x_rows[...], up_t, preferred_element_type=F32)
        back_grad = last_dot(c_rows[...], down_w[columns, :])
        logistic = 1.0 / (1.0 + jnp.exp(-pre_gate))
        slope_one = logistic * (1.0 + pre_gate * (1.0 - logistic))
        slope_two = logistic * (1.0 - logistic) * (2.0 + pre_gate * (1.0 - 2.0 * logistic))
        scale_one = back_grad * slope_one
        scale_two = back_grad * pre_up * slope_two
        one_ref[:, columns] = scale_one
        two_ref[:, columns] = scale_two
        along_gate = jnp.dot(v_rows[...], gate_t, preferred_element_type=F32)
        along_up = jnp.dot(v_rows[...], up_t, preferred_element_type=F32)
        ag_ref[:, columns] = along_gate
        au_ref[:, columns] = along_up
        out_gate[:, columns] = (scale_one * along_up + scale_two * along_gate).astype(BF16)
        out_up[:, columns] = (scale_one * along_gate).astype(BF16)
        return carry

    lax.fori_loop(0, 3, tile, 0)
    results_out(out_gate, out_up, gate_w, up_w, x_rows, swap, (out_a, out_b, out_c))


def first_expert(blocks, gate_w, up_w, down_w):
    message = jax.ShapeDtypeStruct((128, SUB, 256), BF16)
    hidden = jax.ShapeDtypeStruct((384, 768), F32)
    results = pl.pallas_call(
        first_expert_kernel,
        out_shape=[message] * 3 + [hidden] * 4,
        in_specs=[VM] * 3 + [ANY] * 3,
        out_specs=[VM] * 7,
        scratch_shapes=[pltpu.VMEM((4096, 768), BF16)] * 2
        + [pltpu.VMEM((768, 4096), BF16)]
        + [pltpu.VMEM((384, 4096), BF16)] * 3
        + [pltpu.VMEM((384, 768), BF16)] * 2
        + [pltpu.SemaphoreType.DMA((3,))],
        name="first_expert",
        compiler_params=pltpu.CompilerParams(vmem_limit_bytes=62 << 20),
    )(*blocks, gate_w, up_w, down_w)
    return results[:3], results[3:]


def first_scalars(total, entries):
    square = total[0:1, 0:1] / entries
    cross = total[1:2, 0:1] / entries
    image = total[2:3, 0:1] / entries
    norm_square = square + EPSILON
    norm = jnp.sqrt(norm_square)
    alpha = cross / norm_square
    variance = (image - 2.0 * alpha * cross + alpha * alpha * square) / norm_square
    beta = jnp.sqrt(jnp.maximum(variance, 0.0) + EPSILON)
    return {"norm": norm, "alpha": alpha, "beta": beta, "square": square}


def second_expert_kernel(
    entries, in_a, in_b, in_c, total, one_ref, two_ref, ag_ref, au_ref, gate_h, up_h, out_a, out_b, out_c,
    gate_w, up_w, v_rows, out_gate, out_up, sems,
):
    copies = [
        pltpu.make_async_copy(src, dst, sems.at[i])
        for i, (src, dst) in enumerate(((gate_h, gate_w), (up_h, up_w)))
    ]
    for copy in copies:
        copy.start()
    swap = swap_matrix()
    for r, source in enumerate((in_a, in_b, in_c)):
        unpack(source, 0, swap, v_rows, r * 128)
    scalars = first_scalars(total[...], entries)
    scale = 1.0 / (scalars["norm"] * scalars["beta"])
    shift = scalars["alpha"] * scale
    for copy in copies:
        copy.wait()

    def tile(index, carry):
        columns = pl.ds(pl.multiple_of(index * 256, 256), 256)
        along_gate = jnp.dot(v_rows[...], gate_w[:, columns], preferred_element_type=F32)
        along_up = jnp.dot(v_rows[...], up_w[:, columns], preferred_element_type=F32)
        along_gate = along_gate * scale - ag_ref[:, columns] * shift
        along_up = along_up * scale - au_ref[:, columns] * shift
        scale_one = one_ref[:, columns]
        out_gate[:, columns] = (scale_one * along_up + two_ref[:, columns] * along_gate).astype(BF16)
        out_up[:, columns] = (scale_one * along_gate).astype(BF16)
        return carry

    lax.fori_loop(0, 3, tile, 0)
    results_out(out_gate, out_up, gate_w, up_w, v_rows, swap, (out_a, out_b, out_c))


def second_expert(entries, blocks, total, hidden, gate_w, up_w):
    message = jax.ShapeDtypeStruct((128, SUB, 256), BF16)
    return pl.pallas_call(
        functools.partial(second_expert_kernel, entries),
        out_shape=[message] * 3,
        in_specs=[VM] * 8 + [ANY] * 2,
        out_specs=[VM] * 3,
        scratch_shapes=[pltpu.VMEM((4096, 768), BF16)] * 2
        + [pltpu.VMEM((384, 4096), BF16)]
        + [pltpu.VMEM((384, 768), BF16)] * 2
        + [pltpu.SemaphoreType.DMA((2,))],
        name="second_expert",
        compiler_params=pltpu.CompilerParams(vmem_limit_bytes=56 << 20),
    )(*blocks, total, *hidden, gate_w, up_w)


CONTRACT_FIRST = (((0,), (0,)), ((), ()))


def gather_image(blocks, pick_ref, swap, rows, image):
    for r in range(3):
        unpack(blocks[r], 0, swap, rows, r * 128)
    picks = jnp.concatenate([pick_ref[r] for r in range(3)], axis=0)
    for part in range(8):
        columns = slice(part * 512, (part + 1) * 512)
        image[:, columns] = lax.dot_general(picks, rows[:, columns], CONTRACT_FIRST, preferred_element_type=F32)


def as_tile(values):
    row = lax.broadcasted_iota(jnp.int32, (8, 128), 0)
    tile = jnp.zeros((8, 128), F32)
    for index, value in enumerate(values):
        tile = jnp.where(row == index, value, tile)
    return tile


def whole_sum(array):
    return jnp.sum(jnp.sum(array, axis=0, keepdims=True), axis=1, keepdims=True)


def turn_kernel(in_a, in_b, in_c, pick_ref, start, image, out_a, out_b, out_c, part_ref, rows):
    swap = swap_matrix()
    gather_image((in_a, in_b, in_c), pick_ref, swap, rows, image)
    anchor = start[...].astype(F32)
    found = image[...]
    part_ref[...] = as_tile([whole_sum(anchor * anchor), whole_sum(anchor * found), whole_sum(found * found)])
    for part in range(4):
        columns = slice(part * 1024, (part + 1) * 1024)
        narrow = image[:, columns].astype(BF16)
        for r in range(3):
            picked = jnp.dot(pick_ref[r], narrow, preferred_element_type=F32)
            rows[r * 128 : (r + 1) * 128, columns] = picked.astype(BF16)
    for r, out in enumerate((out_a, out_b, out_c)):
        pack(rows, r * 128, swap, out, 0)


def turn(blocks, pick, start):
    message = jax.ShapeDtypeStruct((128, SUB, 256), BF16)
    results = pl.pallas_call(
        turn_kernel,
        out_shape=[jax.ShapeDtypeStruct(start.shape, F32)]
        + [message] * 3
        + [jax.ShapeDtypeStruct((8, 128), F32)],
        in_specs=[VM] * 5,
        out_specs=[VM] * 5,
        scratch_shapes=[pltpu.VMEM((384, 4096), BF16)],
        name="turn",
        compiler_params=pltpu.CompilerParams(vmem_limit_bytes=32 << 20),
    )(*blocks, pick, start)
    return results[0], results[1:4], results[4]


def finish_kernel(
    entries, in_a, in_b, in_c, pick_ref, start, first_image, total_ref, basis_ref, residual_ref, tri_ref,
    rows, image, tile_a, tile_b, tile_c, sum_send, sum_recv,
):
    place = here()
    reduction = Reduction(place, (tile_a, tile_b, tile_c), sum_send, sum_recv)
    peers = []
    for axes in REDUCE_GROUPS:
        peers += [moved(place, axes, step) for step in offsets(axes)[1:]]
    entry_barrier(peers)
    swap = swap_matrix()
    gather_image((in_a, in_b, in_c), pick_ref, swap, rows, image)
    scalars = first_scalars(total_ref[...], entries)
    norm, alpha, beta = scalars["norm"], scalars["alpha"], scalars["beta"]
    base = start[...].astype(F32) / norm
    basis = ((first_image[...] / norm - alpha * base) / beta).astype(BF16)
    basis_ref[...] = basis
    wide = basis.astype(F32)
    found = image[...]
    partial = as_tile(
        [
            whole_sum(wide * found),
            whole_sum(found * found),
            whole_sum(base * found),
            whole_sum(wide * wide),
            whole_sum(wide * base),
            whole_sum(base * base),
        ]
    )
    reduction.send(0, partial)
    reduction.send(1, reduction.receive(0))
    reduction.send(2, reduction.receive(1))
    total = reduction.receive(2) / entries
    alpha_one = total[0:1, 0:1]
    square = (
        total[1:2, 0:1]
        - 2.0 * alpha_one * total[0:1, 0:1]
        - 2.0 * beta * total[2:3, 0:1]
        + alpha_one * alpha_one * total[3:4, 0:1]
        + 2.0 * alpha_one * beta * total[4:5, 0:1]
        + beta * beta * total[5:6, 0:1]
    )
    beta_two = jnp.sqrt(jnp.maximum(square, 0.0) + EPSILON)
    residual_ref[...] = image[...] - alpha_one * basis_ref[...].astype(F32) - beta * (start[...].astype(F32) / norm)
    tri_ref[...] = as_tile([alpha, beta, alpha_one, beta_two])


def finish(entries, blocks, pick, start, first_image, total):
    return pl.pallas_call(
        functools.partial(finish_kernel, entries),
        out_shape=[
            jax.ShapeDtypeStruct(start.shape, BF16),
            jax.ShapeDtypeStruct(start.shape, F32),
            jax.ShapeDtypeStruct((8, 128), F32),
        ],
        in_specs=[VM] * 7,
        out_specs=[VM] * 3,
        scratch_shapes=[pltpu.VMEM((384, 4096), BF16), pltpu.VMEM(start.shape, F32)] + reduction_scratch(),
        name="finish",
        compiler_params=pltpu.CompilerParams(
            collective_id=5, has_side_effects=True, vmem_limit_bytes=32 << 20
        ),
    )(*blocks, pick, start, first_image, total)


def on_device(tokens, cotangent, start, gates, routes, w_gate, w_up, w_down):
    entries = float(128 * tokens.shape[0] * tokens.shape[1])
    gate_w, up_w, down_w = w_gate[0], w_up[0], w_down[0]
    outgoing = send_messages(routes, gates, tokens, cotangent, start)
    blocks, pick = outgoing[:3], outgoing[3]
    arrived = exchange(blocks, False, 0)
    answers, hidden = first_expert(arrived, gate_w, up_w, down_w)
    returned = exchange(answers, True, 1)
    image_zero, blocks, part = turn(returned, pick, start)
    arrived, total = exchange(blocks, False, 2, part)
    answers = second_expert(entries, arrived, total, hidden, gate_w, up_w)
    returned = exchange(answers, True, 3)
    basis, residual, tri = finish(entries, returned, pick, start, image_zero, total)
    return basis, residual, tri[:4, 0]


def solution(mesh):
    rows = P(("dp", "expert"), None)
    experts = P(("dp", "expert"), None, None)
    return jax.shard_map(
        on_device,
        mesh=mesh,
        in_specs=(rows,) * 5 + (experts,) * 3,
        out_specs=(rows, rows, P()),
        check_vma=False,
    )
```

```python
import functools
import jax
import jax.numpy as jnp
from jax import lax
from jax.experimental import pallas as pl
from jax.experimental.pallas import tpu as pltpu
from jax.sharding import PartitionSpec as P

EPSILON = 1e-06
MESH = pl.DeviceIdType.MESH
F32 = jnp.float32
BF16 = jnp.bfloat16
SUB = 16
ORDERS = (("z", "x", "y"), ("x", "y", "z"), ("y", "z", "x"))
ANY = pl.BlockSpec(memory_space=pl.ANY)
VM = pl.BlockSpec(memory_space=pltpu.VMEM)


def rem(value, size):
    return lax.rem(value, jnp.int32(size))


def here():
    expert = lax.axis_index("expert")
    return {
        "z": lax.axis_index("dp"),
        "x": expert // 8,
        "y": rem(expert // 2, 4),
        "c": rem(expert, 2),
    }


def device_of(place):
    return (place["z"], place["x"] * 8 + place["y"] * 2 + place["c"])


def offsets(axes):
    if len(axes) == 1:
        return [(0,), (1,), (3,), (2,)]
    return [(0, 0), (0, 1), (1, 0), (3, 0), (1, 1), (3, 1), (2, 0), (2, 1)]


def size_of(axes):
    return 4 if len(axes) == 1 else 8


def index_of(place, axes):
    value = place[axes[0]]
    return value * 2 + place["c"] if len(axes) == 2 else value


def moved(place, axes, step, sign=1):
    new = dict(place)
    for axis, amount in zip(axes, step):
        count = 2 if axis == "c" else 4
        new[axis] = rem(place[axis] + (amount if sign > 0 else count - amount), count)
    return new


def slot_id(axes, step):
    return step[0] * 2 + step[1] if len(axes) == 2 else step[0]


def groups_of(order, back):
    first, second, third = (order[0],), (order[1],), (order[2], "c")
    return (third, second, first) if back else (first, second, third)


def peers_of(place):
    found = []
    for axis in ("z", "x", "y"):
        for amount in (1, 2, 3):
            near = moved(place, (axis,), (amount,))
            found.append(near)
            found.append(moved(near, ("c",), (1,)))
    found.append(moved(place, ("c",), (1,)))
    return found


def entry_barrier(places):
    barrier = pltpu.get_barrier_semaphore()
    for place in places:
        pl.semaphore_signal(barrier, inc=1, device_id=device_of(place), device_id_type=MESH)
    pl.semaphore_wait(barrier, len(places))


REDUCE_GROUPS = (("z",), ("x",), ("y", "c"))


class Reduction:
    def __init__(self, place, tiles, send_sem, recv_sem):
        self.place, self.tiles = place, tiles
        self.send_sem, self.recv_sem = send_sem, recv_sem

    def send(self, level, value):
        axes, place = REDUCE_GROUPS[level], self.place
        tile = self.tiles[level]
        mine = index_of(place, axes)
        tile[mine] = value
        for step in offsets(axes)[1:]:
            pltpu.make_async_remote_copy(
                tile.at[mine],
                tile.at[mine],
                self.send_sem.at[level],
                self.recv_sem.at[level],
                device_id=device_of(moved(place, axes, step)),
                device_id_type=MESH,
            ).start()

    def receive(self, level):
        axes, place = REDUCE_GROUPS[level], self.place
        tile = self.tiles[level]
        count = size_of(axes)
        rest = tile.at[pl.ds(0, count - 1)]
        bulk = pltpu.make_async_remote_copy(
            rest,
            rest,
            self.send_sem.at[level],
            self.recv_sem.at[level],
            device_id=device_of(moved(place, axes, offsets(axes)[1])),
            device_id_type=MESH,
        )
        bulk.wait_send()
        bulk.wait_recv()
        total = tile[0]
        for index in range(1, count):
            total = total + tile[index]
        return total


def reduction_scratch():
    return [
        pltpu.VMEM((4, 8, 128), F32),
        pltpu.VMEM((4, 8, 128), F32),
        pltpu.VMEM((8, 8, 128), F32),
        pltpu.SemaphoreType.DMA((3,)),
        pltpu.SemaphoreType.DMA((3,)),
    ]


def exchange_kernel(back, summing, *refs):
    blocks = refs[:3]
    refs = refs[3:]
    if summing:
        part, refs = refs[0], refs[1:]
    outs, refs = refs[:3], refs[3:]
    if summing:
        total, refs = refs[0], refs[1:]
    first_hold, second_hold, refs = refs[:3], refs[3:6], refs[6:]
    (send_one, send_two, send_three, recv_one, recv_two, recv_three, local_one, local_two, local_three) = refs[:9]
    place = here()
    plans = [groups_of(order, back) for order in ORDERS]
    if summing:
        tiles, (sum_send, sum_recv) = refs[9:12], refs[12:14]
        reduction = Reduction(place, tiles, sum_send, sum_recv)
    entry_barrier(peers_of(place))

    def remote(src, dst, send_sem, recv_sem, target):
        return pltpu.make_async_remote_copy(
            src, dst, send_sem, recv_sem, device_id=device_of(target), device_id_type=MESH
        )

    if summing:
        reduction.send(0, part[...])
    for turn in range(8):
        for r, (one, two, three) in enumerate(plans):
            if turn >= size_of(one):
                continue
            step = offsets(one)[turn]
            mine = index_of(place, one)
            if turn == 0:
                pltpu.make_async_copy(blocks[r].at[mine], first_hold[r].at[mine], local_one.at[r]).start()
                continue
            target = moved(place, one, step)
            remote(
                blocks[r].at[index_of(target, one)],
                first_hold[r].at[mine],
                send_one.at[r],
                recv_one.at[r, slot_id(one, step)],
                target,
            ).start()
    for turn in range(8):
        for r, (one, two, three) in enumerate(plans):
            if turn >= size_of(one):
                continue
            step = offsets(one)[turn]
            mine_one, mine_two = index_of(place, one), index_of(place, two)
            if turn == 0:
                source = mine_one
                pltpu.make_async_copy(blocks[r].at[source], first_hold[r].at[source], local_one.at[r]).wait()
            else:
                origin = moved(place, one, step, -1)
                source = index_of(origin, one)
                held = first_hold[r].at[source]
                remote(held, held, send_one.at[r], recv_one.at[r, slot_id(one, step)], origin).wait_recv()
            for hop in offsets(two)[1:]:
                target = moved(place, two, hop)
                remote(
                    first_hold[r].at[source, index_of(target, two)],
                    second_hold[r].at[mine_two, source],
                    send_two.at[r],
                    recv_two.at[r, slot_id(two, hop)],
                    target,
                ).start()
            pltpu.make_async_copy(
                first_hold[r].at[source, mine_two], second_hold[r].at[mine_two, source], local_two.at[r]
            ).start()
    if summing:
        reduction.send(1, reduction.receive(0))
    for turn in range(4):
        for r, (one, two, three) in enumerate(plans):
            step = offsets(two)[turn]
            mine_two, mine_three = index_of(place, two), index_of(place, three)
            if turn == 0:
                source = mine_two
                held = second_hold[r].at[source]
                pltpu.make_async_copy(held, held, local_two.at[r]).wait()
            else:
                origin = moved(place, two, step, -1)
                source = index_of(origin, two)
                held = second_hold[r].at[source]
                remote(held, held, send_two.at[r], recv_two.at[r, slot_id(two, step)], origin).wait_recv()
            for hop in offsets(three)[1:]:
                target = moved(place, three, hop)
                remote(
                    second_hold[r].at[source, :, index_of(target, three)],
                    outs[r].at[mine_three, source],
                    send_three.at[r],
                    recv_three.at[r],
                    target,
                ).start()
            pltpu.make_async_copy(
                second_hold[r].at[source, :, mine_three], outs[r].at[mine_three, source], local_three.at[r]
            ).start()
    if summing:
        reduction.send(2, reduction.receive(1))
        total[...] = reduction.receive(2)
    near = moved(place, ("c",), (1,))
    for r, (one, two, three) in enumerate(plans):
        rest = blocks[r].at[pl.ds(0, size_of(one) - 1)]
        remote(rest, rest, send_one.at[r], recv_three.at[r], near).wait_send()
        rest = second_hold[r].at[pl.ds(0, 3)]
        remote(rest, rest, send_two.at[r], recv_three.at[r], near).wait_send()
        rest = outs[r].at[pl.ds(0, size_of(three) - 1)]
        bulk = remote(rest, rest, send_three.at[r], recv_three.at[r], near)
        bulk.wait_send()
        bulk.wait_recv()
        mine = outs[r].at[index_of(place, three)]
        pltpu.make_async_copy(mine, mine, local_three.at[r]).wait()


def exchange(blocks, back, number, part=None):
    sub, lanes = blocks[0].shape[1:]
    dims_in = (8, 4, 4) if back else (4, 4, 8)
    dims_out = dims_in[::-1]
    one, two, three = dims_in
    summing = part is not None
    scratch = [pltpu.VMEM((one, two, three, sub, lanes), BF16)] * 3
    scratch += [pltpu.VMEM((two, one, three, sub, lanes), BF16)] * 3
    scratch += [pltpu.SemaphoreType.DMA((3,))] * 3
    scratch += [pltpu.SemaphoreType.DMA((3, 8))] * 2
    scratch += [pltpu.SemaphoreType.DMA((3,))] * 4
    out_shape = [jax.ShapeDtypeStruct(dims_out + (sub, lanes), BF16)] * 3
    operands = [block.reshape(dims_in + (sub, lanes)) for block in blocks]
    in_specs, out_specs = [ANY] * 3, [ANY] * 3
    if summing:
        operands.append(part)
        in_specs.append(VM)
        out_specs.append(VM)
        out_shape.append(jax.ShapeDtypeStruct((8, 128), F32))
        scratch += reduction_scratch()
    results = pl.pallas_call(
        functools.partial(exchange_kernel, back, summing),
        out_shape=out_shape,
        in_specs=in_specs,
        out_specs=out_specs,
        scratch_shapes=scratch,
        name="exchange_%d" % number,
        compiler_params=pltpu.CompilerParams(
            collective_id=number, has_side_effects=True, vmem_limit_bytes=48 << 20
        ),
    )(*operands)
    moved_blocks = [result.reshape(128, sub, lanes) for result in results[:3]]
    return (moved_blocks, results[3]) if summing else moved_blocks


def swap_matrix():
    row = lax.broadcasted_iota(jnp.int32, (256, 256), 0)
    column = lax.broadcasted_iota(jnp.int32, (256, 256), 1)
    hit = (row // 16 == rem(column, 16)) & (rem(row, 16) == column // 16)
    return hit.astype(F32).astype(BF16)


def pack(rows_ref, row_start, swap, out_ref, lane):
    def block(index, carry):
        start = pl.multiple_of(row_start + index * 16, 16)
        stacked = jnp.concatenate(
            [rows_ref[pl.ds(start, 16), j * 256 : (j + 1) * 256] for j in range(SUB)], axis=0
        )
        turned = jnp.dot(swap, stacked, preferred_element_type=F32).astype(BF16)
        out_ref[pl.ds(pl.multiple_of(index * 16, 16), 16), :, lane : lane + 256] = turned.reshape(16, 16, 256)
        return carry

    lax.fori_loop(0, 8, block, 0)


def unpack(in_ref, lane, swap, rows_ref, row_start):
    def block(index, carry):
        stacked = in_ref[pl.ds(pl.multiple_of(index * 16, 16), 16), :, lane : lane + 256].reshape(256, 256)
        turned = jnp.dot(swap, stacked, preferred_element_type=F32).astype(BF16)
        start = pl.multiple_of(row_start + index * 16, 16)
        for j in range(SUB):
            rows_ref[pl.ds(start, 16), j * 256 : (j + 1) * 256] = turned[j * 16 : (j + 1) * 16, :]
        return carry

    lax.fori_loop(0, 8, block, 0)


def expert_ids(order):
    position = lax.broadcasted_iota(jnp.int32, (128, 32), 0)
    value = {
        order[0]: position // 32,
        order[1]: rem(position // 8, 4),
        order[2]: rem(position // 2, 4),
    }
    return value["z"] * 32 + value["x"] * 8 + value["y"] * 2 + rem(position, 2)


def own_picks(table, pick_ref, early):
    for r in range(3):
        ids = expert_ids(ORDERS[r]).astype(F32)
        named = jnp.zeros((128, 32), F32)
        for k in range(8):
            named = named + (table[k : k + 1, 0:32] == ids).astype(F32)
        before = jnp.dot(named.astype(BF16), early, preferred_element_type=F32)
        keep = (named > 0.5) & (before == float(r))
        pick_ref[r] = keep.astype(F32).astype(BF16)


def scatter_kernel(
    tokens, cotangent, start, table_ref, out_a, out_b, out_c, pick_ref,
    held, tables, first_a, first_b, first_c, second_a, second_b, second_c, rows,
    row_send, row_recv, tab_send, tab_recv, send_two, recv_two, local_two, send_three, recv_three, local_three,
):
    sources, outs = (tokens, cotangent, start), (out_a, out_b, out_c)
    first_hold, second_hold = (first_a, first_b, first_c), (second_a, second_b, second_c)
    place = here()
    plans = [groups_of(order, False) for order in ORDERS]
    entry_barrier(peers_of(place))

    def remote(src, dst, send_sem, recv_sem, target):
        return pltpu.make_async_remote_copy(
            src, dst, send_sem, recv_sem, device_id=device_of(target), device_id_type=MESH
        )

    for step in offsets(("z",))[1:]:
        for u, (one, two, three) in enumerate(plans):
            mine, target, slot = index_of(place, one), moved(place, one, step), slot_id(one, step)
            remote(table_ref, tables.at[u, mine], tab_send.at[u], tab_recv.at[u, slot], target).start()
            remote(sources[u], held.at[u, mine], row_send.at[u], row_recv.at[u, slot], target).start()

    swap = swap_matrix()
    early = lax.broadcasted_iota(jnp.int32, (32, 32), 0) < lax.broadcasted_iota(jnp.int32, (32, 32), 1)
    early = early.astype(F32).astype(BF16)
    position = lax.broadcasted_iota(jnp.int32, (32, 32), 0)

    def origin_of(turn, u):
        step = offsets(plans[u][0])[turn]
        return step, moved(place, plans[u][0], step, -1)

    def build(turn, u, between):
        order = ORDERS[u]
        step, origin = origin_of(turn, u)
        source = place[order[0]] if turn == 0 else origin[order[0]]
        if turn == 0:
            table, block = table_ref, sources[u]
        else:
            table, block = tables.at[u, source], held.at[u, source]
            remote(table, table, tab_send.at[u], tab_recv.at[u, step[0]], origin).wait_recv()
            remote(block, block, row_send.at[u], row_recv.at[u, step[0]], origin).wait_recv()
        value = {order[0]: place[order[0]], order[1]: position // 8, order[2]: rem(position // 2, 4)}
        ids = (value["z"] * 32 + value["x"] * 8 + value["y"] * 2 + rem(position, 2)).astype(F32)
        named = jnp.zeros((32, 32), F32)
        weight = jnp.zeros((32, 32), F32)
        for k in range(8):
            hit = table[k : k + 1, 0:32] == ids
            named = named + hit.astype(F32)
            weight = weight + jnp.where(hit, table[8 + k : 9 + k, 0:32], 0.0)
        before = jnp.dot(named.astype(BF16), early, preferred_element_type=F32)
        keeps = [((named > 0.5) & (before == float(r))).astype(F32) for r in range(3)]
        pick = jnp.concatenate(keeps, axis=0)
        slot_gate = jnp.sum(pick * jnp.concatenate([weight] * 3, axis=0), axis=1, keepdims=True)
        pick = pick.astype(BF16)
        for part in range(4):
            columns = slice(part * 1024, (part + 1) * 1024)
            picked = jnp.dot(pick, block[:, columns], preferred_element_type=F32)
            if u == 1:
                picked = picked * slot_gate
            rows[:, columns] = picked.astype(BF16)
        between()

        def turned(r, carry):
            lanes = pl.ds(pl.multiple_of(r * 256, 256), 256)
            for half in range(2):
                begin = pl.multiple_of(r * 32 + half * 16, 16)
                stacked = jnp.concatenate(
                    [rows[pl.ds(begin, 16), j * 256 : (j + 1) * 256] for j in range(SUB)], axis=0
                )
                tile = jnp.dot(swap, stacked, preferred_element_type=F32).astype(BF16)
                first_hold[u][source, half * 2 : half * 2 + 2, :, :, lanes] = tile.reshape(2, 8, SUB, 256)
            return carry

        lax.fori_loop(0, 3, turned, 0)

    def send(turn, u):
        one, two, three = plans[u]
        source = index_of(origin_of(turn, u)[1], one) if turn else index_of(place, one)
        mine_two = index_of(place, two)
        for hop in offsets(two)[1:]:
            target = moved(place, two, hop)
            remote(
                first_hold[u].at[source, index_of(target, two)],
                second_hold[u].at[mine_two, source],
                send_two.at[u],
                recv_two.at[u, slot_id(two, hop)],
                target,
            ).start()
        pltpu.make_async_copy(
            first_hold[u].at[source, mine_two], second_hold[u].at[mine_two, source], local_two.at[u]
        ).start()

    chunks = [(turn, u) for turn in range(4) for u in range(3)]
    for index, chunk in enumerate(chunks):
        build(*chunk, (lambda: None) if index == 0 else functools.partial(send, *chunks[index - 1]))
    own_picks(table_ref, pick_ref, early)
    send(*chunks[-1])
    for turn in range(4):
        for u, (one, two, three) in enumerate(plans):
            step = offsets(two)[turn]
            mine_two, mine_three = index_of(place, two), index_of(place, three)
            if turn == 0:
                source = mine_two
                block = second_hold[u].at[source]
                pltpu.make_async_copy(block, block, local_two.at[u]).wait()
            else:
                origin = moved(place, two, step, -1)
                source = index_of(origin, two)
                block = second_hold[u].at[source]
                remote(block, block, send_two.at[u], recv_two.at[u, slot_id(two, step)], origin).wait_recv()
            for hop in offsets(three)[1:]:
                target = moved(place, three, hop)
                remote(
                    second_hold[u].at[source, :, index_of(target, three)],
                    outs[u].at[mine_three, source],
                    send_three.at[u],
                    recv_three.at[u],
                    target,
                ).start()
            pltpu.make_async_copy(
                second_hold[u].at[source, :, mine_three], outs[u].at[mine_three, source], local_three.at[u]
            ).start()
    near = moved(place, ("c",), (1,))
    for u, (one, two, three) in enumerate(plans):
        rest = tables.at[u, pl.ds(0, 3)]
        remote(rest, rest, tab_send.at[u], recv_three.at[u], near).wait_send()
        rest = held.at[u, pl.ds(0, 3)]
        remote(rest, rest, row_send.at[u], recv_three.at[u], near).wait_send()
        rest = second_hold[u].at[pl.ds(0, 3)]
        remote(rest, rest, send_two.at[u], recv_three.at[u], near).wait_send()
        rest = outs[u].at[pl.ds(0, 7)]
        bulk = remote(rest, rest, send_three.at[u], recv_three.at[u], near)
        bulk.wait_send()
        bulk.wait_recv()
        mine = outs[u].at[index_of(place, three)]
        pltpu.make_async_copy(mine, mine, local_three.at[u]).wait()


def scatter(routes, gates, tokens, cotangent, start):
    table = jnp.concatenate([routes.T.astype(F32), gates.T], axis=0)
    table = jnp.pad(table, ((0, 0), (0, 96)))
    results = pl.pallas_call(
        scatter_kernel,
        out_shape=[jax.ShapeDtypeStruct((8, 4, 4, SUB, 768), BF16)] * 3
        + [jax.ShapeDtypeStruct((3, 128, 32), BF16)],
        in_specs=[VM] * 4,
        out_specs=[ANY] * 3 + [VM],
        scratch_shapes=[pltpu.VMEM((3, 4, 32, 4096), BF16), pltpu.VMEM((3, 4, 16, 128), F32)]
        + [pltpu.VMEM((4, 4, 8, SUB, 768), BF16)] * 6
        + [pltpu.VMEM((96, 4096), BF16)]
        + [pltpu.SemaphoreType.DMA((3,)), pltpu.SemaphoreType.DMA((3, 4))] * 2
        + [pltpu.SemaphoreType.DMA((3,)), pltpu.SemaphoreType.DMA((3, 8))]
        + [pltpu.SemaphoreType.DMA((3,))] * 4,
        name="scatter",
        compiler_params=pltpu.CompilerParams(
            collective_id=0, has_side_effects=True, vmem_limit_bytes=48 << 20
        ),
    )(tokens, cotangent, start, table)
    return [result.reshape(128, SUB, 768) for result in results[:3]], results[3]


def unpack_unit(in_ref, u, r, swap, rows_ref):
    order, home = ORDERS[r], ORDERS[u]

    def block(index, carry):
        pieces = []
        for spot in range(16):
            value = {order[2]: index // 2, order[1]: spot // 4, order[0]: spot % 4}
            third = value[home[2]] * 2 + rem(index, 2)
            pieces.append(in_ref[third * 16 + value[home[1]] * 4 + value[home[0]], :, r * 256 : (r + 1) * 256])
        stacked = jnp.concatenate(pieces, axis=0)
        turned = jnp.dot(swap, stacked, preferred_element_type=F32).astype(BF16)
        start = pl.multiple_of(r * 128 + index * 16, 16)
        for j in range(SUB):
            rows_ref[pl.ds(start, 16), j * 256 : (j + 1) * 256] = turned[j * 16 : (j + 1) * 16, :]
        return carry

    lax.fori_loop(0, 8, block, 0)


CONTRACT_LAST = (((1,), (1,)), ((), ()))


def last_dot(left, right):
    return lax.dot_general(left, right, CONTRACT_LAST, preferred_element_type=F32)


def results_out(out_gate, out_up, gate_w, up_w, rows, swap, outs):
    def tile(index, carry):
        start = pl.multiple_of(index * 256, 256)
        summed = last_dot(out_gate[...], gate_w[pl.ds(start, 256), :])
        summed = summed + last_dot(out_up[...], up_w[pl.ds(start, 256), :])
        rows[:, pl.ds(start, 256)] = summed.astype(BF16)
        return carry

    lax.fori_loop(0, 16, tile, 0)
    for r in range(3):
        pack(rows, r * 128, swap, outs[r], 0)


def first_expert_kernel(
    in_a, in_b, in_c, gate_h, up_h, down_h, out_a, out_b, out_c, one_ref, two_ref, ag_ref, au_ref,
    gate_w, up_w, down_w, x_rows, c_rows, v_rows, out_gate, out_up, sems,
):
    copies = [
        pltpu.make_async_copy(src, dst, sems.at[i])
        for i, (src, dst) in enumerate(((gate_h, gate_w), (up_h, up_w), (down_h, down_w)))
    ]
    for copy in copies:
        copy.start()
    swap = swap_matrix()
    for u, (source, rows) in enumerate(((in_a, x_rows), (in_b, c_rows), (in_c, v_rows))):
        for r in range(3):
            unpack_unit(source, u, r, swap, rows)
    for copy in copies:
        copy.wait()

    def tile(index, carry):
        columns = pl.ds(pl.multiple_of(index * 256, 256), 256)
        gate_t, up_t = gate_w[:, columns], up_w[:, columns]
        pre_gate = jnp.dot(x_rows[...], gate_t, preferred_element_type=F32)
        pre_up = jnp.dot(x_rows[...], up_t, preferred_element_type=F32)
        back_grad = last_dot(c_rows[...], down_w[columns, :])
        logistic = 1.0 / (1.0 + jnp.exp(-pre_gate))
        slope_one = logistic * (1.0 + pre_gate * (1.0 - logistic))
        slope_two = logistic * (1.0 - logistic) * (2.0 + pre_gate * (1.0 - 2.0 * logistic))
        scale_one = back_grad * slope_one
        scale_two = back_grad * pre_up * slope_two
        one_ref[:, columns] = scale_one
        two_ref[:, columns] = scale_two
        along_gate = jnp.dot(v_rows[...], gate_t, preferred_element_type=F32)
        along_up = jnp.dot(v_rows[...], up_t, preferred_element_type=F32)
        ag_ref[:, columns] = along_gate
        au_ref[:, columns] = along_up
        out_gate[:, columns] = (scale_one * along_up + scale_two * along_gate).astype(BF16)
        out_up[:, columns] = (scale_one * along_gate).astype(BF16)
        return carry

    lax.fori_loop(0, 3, tile, 0)
    results_out(out_gate, out_up, gate_w, up_w, x_rows, swap, (out_a, out_b, out_c))


def first_expert(blocks, gate_w, up_w, down_w):
    message = jax.ShapeDtypeStruct((128, SUB, 256), BF16)
    hidden = jax.ShapeDtypeStruct((384, 768), F32)
    results = pl.pallas_call(
        first_expert_kernel,
        out_shape=[message] * 3 + [hidden] * 4,
        in_specs=[VM] * 3 + [ANY] * 3,
        out_specs=[VM] * 7,
        scratch_shapes=[pltpu.VMEM((4096, 768), BF16)] * 2
        + [pltpu.VMEM((768, 4096), BF16)]
        + [pltpu.VMEM((384, 4096), BF16)] * 3
        + [pltpu.VMEM((384, 768), BF16)] * 2
        + [pltpu.SemaphoreType.DMA((3,))],
        name="first_expert",
        compiler_params=pltpu.CompilerParams(vmem_limit_bytes=62 << 20),
    )(*blocks, gate_w, up_w, down_w)
    return results[:3], results[3:]


def first_scalars(total, entries):
    square = total[0:1, 0:1] / entries
    cross = total[1:2, 0:1] / entries
    image = total[2:3, 0:1] / entries
    norm_square = square + EPSILON
    norm = jnp.sqrt(norm_square)
    alpha = cross / norm_square
    variance = (image - 2.0 * alpha * cross + alpha * alpha * square) / norm_square
    beta = jnp.sqrt(jnp.maximum(variance, 0.0) + EPSILON)
    return {"norm": norm, "alpha": alpha, "beta": beta, "square": square}


def second_expert_kernel(
    entries, in_a, in_b, in_c, total, one_ref, two_ref, ag_ref, au_ref, gate_h, up_h, out_a, out_b, out_c,
    gate_w, up_w, v_rows, out_gate, out_up, sems,
):
    copies = [
        pltpu.make_async_copy(src, dst, sems.at[i])
        for i, (src, dst) in enumerate(((gate_h, gate_w), (up_h, up_w)))
    ]
    for copy in copies:
        copy.start()
    swap = swap_matrix()
    for r, source in enumerate((in_a, in_b, in_c)):
        unpack(source, 0, swap, v_rows, r * 128)
    scalars = first_scalars(total[...], entries)
    scale = 1.0 / (scalars["norm"] * scalars["beta"])
    shift = scalars["alpha"] * scale
    for copy in copies:
        copy.wait()

    def tile(index, carry):
        columns = pl.ds(pl.multiple_of(index * 256, 256), 256)
        along_gate = jnp.dot(v_rows[...], gate_w[:, columns], preferred_element_type=F32)
        along_up = jnp.dot(v_rows[...], up_w[:, columns], preferred_element_type=F32)
        along_gate = along_gate * scale - ag_ref[:, columns] * shift
        along_up = along_up * scale - au_ref[:, columns] * shift
        scale_one = one_ref[:, columns]
        out_gate[:, columns] = (scale_one * along_up + two_ref[:, columns] * along_gate).astype(BF16)
        out_up[:, columns] = (scale_one * along_gate).astype(BF16)
        return carry

    lax.fori_loop(0, 3, tile, 0)
    results_out(out_gate, out_up, gate_w, up_w, v_rows, swap, (out_a, out_b, out_c))


def second_expert(entries, blocks, total, hidden, gate_w, up_w):
    message = jax.ShapeDtypeStruct((128, SUB, 256), BF16)
    return pl.pallas_call(
        functools.partial(second_expert_kernel, entries),
        out_shape=[message] * 3,
        in_specs=[VM] * 8 + [ANY] * 2,
        out_specs=[VM] * 3,
        scratch_shapes=[pltpu.VMEM((4096, 768), BF16)] * 2
        + [pltpu.VMEM((384, 4096), BF16)]
        + [pltpu.VMEM((384, 768), BF16)] * 2
        + [pltpu.SemaphoreType.DMA((2,))],
        name="second_expert",
        compiler_params=pltpu.CompilerParams(vmem_limit_bytes=56 << 20),
    )(*blocks, total, *hidden, gate_w, up_w)


CONTRACT_FIRST = (((0,), (0,)), ((), ()))


def gather_image(blocks, pick_ref, swap, rows, image):
    for r in range(3):
        unpack(blocks[r], 0, swap, rows, r * 128)
    picks = jnp.concatenate([pick_ref[r] for r in range(3)], axis=0)
    for part in range(8):
        columns = slice(part * 512, (part + 1) * 512)
        image[:, columns] = lax.dot_general(picks, rows[:, columns], CONTRACT_FIRST, preferred_element_type=F32)


def as_tile(values):
    row = lax.broadcasted_iota(jnp.int32, (8, 128), 0)
    tile = jnp.zeros((8, 128), F32)
    for index, value in enumerate(values):
        tile = jnp.where(row == index, value, tile)
    return tile


def whole_sum(array):
    return jnp.sum(jnp.sum(array, axis=0, keepdims=True), axis=1, keepdims=True)


def turn_kernel(in_a, in_b, in_c, pick_ref, start, image, out_a, out_b, out_c, part_ref, rows):
    swap = swap_matrix()
    gather_image((in_a, in_b, in_c), pick_ref, swap, rows, image)
    anchor = start[...].astype(F32)
    found = image[...]
    part_ref[...] = as_tile([whole_sum(anchor * anchor), whole_sum(anchor * found), whole_sum(found * found)])
    for part in range(4):
        columns = slice(part * 1024, (part + 1) * 1024)
        narrow = image[:, columns].astype(BF16)
        for r in range(3):
            picked = jnp.dot(pick_ref[r], narrow, preferred_element_type=F32)
            rows[r * 128 : (r + 1) * 128, columns] = picked.astype(BF16)
    for r, out in enumerate((out_a, out_b, out_c)):
        pack(rows, r * 128, swap, out, 0)


def turn(blocks, pick, start):
    message = jax.ShapeDtypeStruct((128, SUB, 256), BF16)
    results = pl.pallas_call(
        turn_kernel,
        out_shape=[jax.ShapeDtypeStruct(start.shape, F32)]
        + [message] * 3
        + [jax.ShapeDtypeStruct((8, 128), F32)],
        in_specs=[VM] * 5,
        out_specs=[VM] * 5,
        scratch_shapes=[pltpu.VMEM((384, 4096), BF16)],
        name="turn",
        compiler_params=pltpu.CompilerParams(vmem_limit_bytes=32 << 20),
    )(*blocks, pick, start)
    return results[0], results[1:4], results[4]


def finish_kernel(
    entries, in_a, in_b, in_c, pick_ref, start, first_image, total_ref, basis_ref, residual_ref, tri_ref,
    rows, image, tile_a, tile_b, tile_c, sum_send, sum_recv,
):
    place = here()
    reduction = Reduction(place, (tile_a, tile_b, tile_c), sum_send, sum_recv)
    peers = []
    for axes in REDUCE_GROUPS:
        peers += [moved(place, axes, step) for step in offsets(axes)[1:]]
    entry_barrier(peers)
    swap = swap_matrix()
    gather_image((in_a, in_b, in_c), pick_ref, swap, rows, image)
    scalars = first_scalars(total_ref[...], entries)
    norm, alpha, beta = scalars["norm"], scalars["alpha"], scalars["beta"]
    base = start[...].astype(F32) / norm
    basis = ((first_image[...] / norm - alpha * base) / beta).astype(BF16)
    basis_ref[...] = basis
    wide = basis.astype(F32)
    found = image[...]
    partial = as_tile(
        [
            whole_sum(wide * found),
            whole_sum(found * found),
            whole_sum(base * found),
            whole_sum(wide * wide),
            whole_sum(wide * base),
            whole_sum(base * base),
        ]
    )
    reduction.send(0, partial)
    reduction.send(1, reduction.receive(0))
    reduction.send(2, reduction.receive(1))
    total = reduction.receive(2) / entries
    alpha_one = total[0:1, 0:1]
    square = (
        total[1:2, 0:1]
        - 2.0 * alpha_one * total[0:1, 0:1]
        - 2.0 * beta * total[2:3, 0:1]
        + alpha_one * alpha_one * total[3:4, 0:1]
        + 2.0 * alpha_one * beta * total[4:5, 0:1]
        + beta * beta * total[5:6, 0:1]
    )
    beta_two = jnp.sqrt(jnp.maximum(square, 0.0) + EPSILON)
    residual_ref[...] = image[...] - alpha_one * basis_ref[...].astype(F32) - beta * (start[...].astype(F32) / norm)
    tri_ref[...] = as_tile([alpha, beta, alpha_one, beta_two])


def finish(entries, blocks, pick, start, first_image, total):
    return pl.pallas_call(
        functools.partial(finish_kernel, entries),
        out_shape=[
            jax.ShapeDtypeStruct(start.shape, BF16),
            jax.ShapeDtypeStruct(start.shape, F32),
            jax.ShapeDtypeStruct((8, 128), F32),
        ],
        in_specs=[VM] * 7,
        out_specs=[VM] * 3,
        scratch_shapes=[pltpu.VMEM((384, 4096), BF16), pltpu.VMEM(start.shape, F32)] + reduction_scratch(),
        name="finish",
        compiler_params=pltpu.CompilerParams(
            collective_id=5, has_side_effects=True, vmem_limit_bytes=32 << 20
        ),
    )(*blocks, pick, start, first_image, total)


def on_device(tokens, cotangent, start, gates, routes, w_gate, w_up, w_down):
    entries = float(128 * tokens.shape[0] * tokens.shape[1])
    gate_w, up_w, down_w = w_gate[0], w_up[0], w_down[0]
    arrived, pick = scatter(routes, gates, tokens, cotangent, start)
    answers, hidden = first_expert(arrived, gate_w, up_w, down_w)
    returned = exchange(answers, True, 1)
    image_zero, blocks, part = turn(returned, pick, start)
    arrived, total = exchange(blocks, False, 2, part)
    answers = second_expert(entries, arrived, total, hidden, gate_w, up_w)
    returned = exchange(answers, True, 3)
    basis, residual, tri = finish(entries, returned, pick, start, image_zero, total)
    return basis, residual, tri[:4, 0]


def solution(mesh):
    rows = P(("dp", "expert"), None)
    experts = P(("dp", "expert"), None, None)
    return jax.shard_map(
        on_device,
        mesh=mesh,
        in_specs=(rows,) * 5 + (experts,) * 3,
        out_specs=(rows, rows, P()),
        check_vma=False,
    )
```

```python
import functools
import jax
import jax.numpy as jnp
from jax import lax
from jax.experimental import pallas as pl
from jax.experimental.pallas import tpu as pltpu
from jax.sharding import PartitionSpec as P

EPSILON = 1e-06
MESH = pl.DeviceIdType.MESH
F32 = jnp.float32
BF16 = jnp.bfloat16
SUB = 16
ORDERS = (("z", "x", "y"), ("x", "y", "z"), ("y", "z", "x"))
ANY = pl.BlockSpec(memory_space=pl.ANY)
VM = pl.BlockSpec(memory_space=pltpu.VMEM)


def rem(value, size):
    return lax.rem(value, jnp.int32(size))


def here():
    expert = lax.axis_index("expert")
    return {
        "z": lax.axis_index("dp"),
        "x": expert // 8,
        "y": rem(expert // 2, 4),
        "c": rem(expert, 2),
    }


def device_of(place):
    return (place["z"], place["x"] * 8 + place["y"] * 2 + place["c"])


def offsets(axes):
    if len(axes) == 1:
        return [(0,), (1,), (3,), (2,)]
    return [(0, 0), (0, 1), (1, 0), (3, 0), (1, 1), (3, 1), (2, 0), (2, 1)]


def size_of(axes):
    return 4 if len(axes) == 1 else 8


def index_of(place, axes):
    value = place[axes[0]]
    return value * 2 + place["c"] if len(axes) == 2 else value


def moved(place, axes, step, sign=1):
    new = dict(place)
    for axis, amount in zip(axes, step):
        count = 2 if axis == "c" else 4
        new[axis] = rem(place[axis] + (amount if sign > 0 else count - amount), count)
    return new


def slot_id(axes, step):
    return step[0] * 2 + step[1] if len(axes) == 2 else step[0]


def groups_of(order, back):
    first, second, third = (order[0],), (order[1],), (order[2], "c")
    return (third, second, first) if back else (first, second, third)


def peers_of(place):
    found = []
    for axis in ("z", "x", "y"):
        for amount in (1, 2, 3):
            near = moved(place, (axis,), (amount,))
            found.append(near)
            found.append(moved(near, ("c",), (1,)))
    found.append(moved(place, ("c",), (1,)))
    return found


def greet(places):
    barrier = pltpu.get_barrier_semaphore()
    for place in places:
        pl.semaphore_signal(barrier, inc=1, device_id=device_of(place), device_id_type=MESH)


def await_greetings(places):
    pl.semaphore_wait(pltpu.get_barrier_semaphore(), len(places))


def entry_barrier(places):
    greet(places)
    await_greetings(places)


REDUCE_GROUPS = (("z",), ("x",), ("y", "c"))


class Reduction:
    def __init__(self, place, tiles, send_sem, recv_sem):
        self.place, self.tiles = place, tiles
        self.send_sem, self.recv_sem = send_sem, recv_sem

    def send(self, level, value):
        axes, place = REDUCE_GROUPS[level], self.place
        tile = self.tiles[level]
        mine = index_of(place, axes)
        tile[mine] = value
        for step in offsets(axes)[1:]:
            pltpu.make_async_remote_copy(
                tile.at[mine],
                tile.at[mine],
                self.send_sem.at[level],
                self.recv_sem.at[level],
                device_id=device_of(moved(place, axes, step)),
                device_id_type=MESH,
            ).start()

    def receive(self, level):
        axes, place = REDUCE_GROUPS[level], self.place
        tile = self.tiles[level]
        count = size_of(axes)
        rest = tile.at[pl.ds(0, count - 1)]
        bulk = pltpu.make_async_remote_copy(
            rest,
            rest,
            self.send_sem.at[level],
            self.recv_sem.at[level],
            device_id=device_of(moved(place, axes, offsets(axes)[1])),
            device_id_type=MESH,
        )
        bulk.wait_send()
        bulk.wait_recv()
        total = tile[0]
        for index in range(1, count):
            total = total + tile[index]
        return total


def reduction_scratch():
    return [
        pltpu.VMEM((4, 8, 128), F32),
        pltpu.VMEM((4, 8, 128), F32),
        pltpu.VMEM((8, 8, 128), F32),
        pltpu.SemaphoreType.DMA((3,)),
        pltpu.SemaphoreType.DMA((3,)),
    ]


def exchange_steps(place, back, make, outs, net, reduction=None, part=None):
    blocks, first_hold, second_hold = net[:3], net[3:6], net[6:9]
    (send_one, send_two, send_three, recv_one, recv_two, recv_three, local_one, local_two, local_three) = net[9:18]
    plans = [groups_of(order, back) for order in ORDERS]
    summing = reduction is not None

    def remote(src, dst, send_sem, recv_sem, target):
        return pltpu.make_async_remote_copy(
            src, dst, send_sem, recv_sem, device_id=device_of(target), device_id_type=MESH
        )

    def launch(turn, r):
        one = plans[r][0]
        step = offsets(one)[turn]
        mine = index_of(place, one)
        if turn == 0:
            pltpu.make_async_copy(blocks[r].at[mine], first_hold[r].at[mine], local_one.at[r]).start()
            return
        target = moved(place, one, step)
        remote(
            blocks[r].at[index_of(target, one)],
            first_hold[r].at[mine],
            send_one.at[r],
            recv_one.at[r, slot_id(one, step)],
            target,
        ).start()

    if summing:
        reduction.send(0, part)
    chunks = [
        (turn, r) for turn in (1, 2, 3, 4, 5, 6, 7, 0) for r in range(3) if turn < size_of(plans[r][0])
    ]
    for number, (turn, r) in enumerate(chunks):
        one = plans[r][0]
        target = moved(place, one, offsets(one)[turn])
        make(r, index_of(target, one), blocks[r])
        if number:
            launch(*chunks[number - 1])
    launch(*chunks[-1])
    for turn in range(8):
        for r, (one, two, three) in enumerate(plans):
            if turn >= size_of(one):
                continue
            step = offsets(one)[turn]
            mine_one, mine_two = index_of(place, one), index_of(place, two)
            if turn == 0:
                source = mine_one
                pltpu.make_async_copy(blocks[r].at[source], first_hold[r].at[source], local_one.at[r]).wait()
            else:
                origin = moved(place, one, step, -1)
                source = index_of(origin, one)
                held = first_hold[r].at[source]
                remote(held, held, send_one.at[r], recv_one.at[r, slot_id(one, step)], origin).wait_recv()
            for hop in offsets(two)[1:]:
                target = moved(place, two, hop)
                remote(
                    first_hold[r].at[source, index_of(target, two)],
                    second_hold[r].at[mine_two, source],
                    send_two.at[r],
                    recv_two.at[r, slot_id(two, hop)],
                    target,
                ).start()
            pltpu.make_async_copy(
                first_hold[r].at[source, mine_two], second_hold[r].at[mine_two, source], local_two.at[r]
            ).start()
    if summing:
        reduction.send(1, reduction.receive(0))
    for turn in range(4):
        for r, (one, two, three) in enumerate(plans):
            step = offsets(two)[turn]
            mine_two, mine_three = index_of(place, two), index_of(place, three)
            if turn == 0:
                source = mine_two
                held = second_hold[r].at[source]
                pltpu.make_async_copy(held, held, local_two.at[r]).wait()
            else:
                origin = moved(place, two, step, -1)
                source = index_of(origin, two)
                held = second_hold[r].at[source]
                remote(held, held, send_two.at[r], recv_two.at[r, slot_id(two, step)], origin).wait_recv()
            for hop in offsets(three)[1:]:
                target = moved(place, three, hop)
                remote(
                    second_hold[r].at[source, :, index_of(target, three)],
                    outs[r].at[mine_three, source],
                    send_three.at[r],
                    recv_three.at[r],
                    target,
                ).start()
            pltpu.make_async_copy(
                second_hold[r].at[source, :, mine_three], outs[r].at[mine_three, source], local_three.at[r]
            ).start()
    if summing:
        reduction.send(2, reduction.receive(1))
        total = reduction.receive(2)
    near = moved(place, ("c",), (1,))
    for r, (one, two, three) in enumerate(plans):
        rest = blocks[r].at[pl.ds(0, size_of(one) - 1)]
        remote(rest, rest, send_one.at[r], recv_three.at[r], near).wait_send()
        rest = second_hold[r].at[pl.ds(0, 3)]
        remote(rest, rest, send_two.at[r], recv_three.at[r], near).wait_send()
        rest = outs[r].at[pl.ds(0, size_of(three) - 1)]
        bulk = remote(rest, rest, send_three.at[r], recv_three.at[r], near)
        bulk.wait_send()
        bulk.wait_recv()
        mine = outs[r].at[index_of(place, three)]
        pltpu.make_async_copy(mine, mine, local_three.at[r]).wait()
    return total if summing else None


def net_scratch(back):
    dims = (8, 4, 4) if back else (4, 4, 8)
    held = (dims[1], dims[0], dims[2])
    scratch = [pltpu.VMEM(dims + (SUB, 256), BF16)] * 6 + [pltpu.VMEM(held + (SUB, 256), BF16)] * 3
    scratch += [pltpu.SemaphoreType.DMA((3,))] * 3
    scratch += [pltpu.SemaphoreType.DMA((3, 8))] * 2
    return scratch + [pltpu.SemaphoreType.DMA((3,))] * 4


def arriving(back):
    dims = (4, 4, 8) if back else (8, 4, 4)
    return [jax.ShapeDtypeStruct(dims + (SUB, 256), BF16)] * 3


def as_messages(blocks):
    return [block.reshape(128, SUB, 256) for block in blocks]


def swap_matrix():
    row = lax.broadcasted_iota(jnp.int32, (256, 256), 0)
    column = lax.broadcasted_iota(jnp.int32, (256, 256), 1)
    hit = (row // 16 == rem(column, 16)) & (rem(row, 16) == column // 16)
    return hit.astype(F32).astype(BF16)


def turned_rows(rows_ref, start, swap):
    start = pl.multiple_of(start, 16)
    stacked = jnp.concatenate(
        [rows_ref[pl.ds(start, 16), j * 256 : (j + 1) * 256] for j in range(SUB)], axis=0
    )
    return jnp.dot(swap, stacked, preferred_element_type=F32).astype(BF16)


def maker(back, rows_ref, swap):
    def make(r, index, block):
        if back:
            block[index] = turned_rows(rows_ref, r * 128 + index * 16, swap).reshape(4, 4, SUB, 256)
            return
        for half in range(2):
            turned = turned_rows(rows_ref, r * 128 + index * 32 + half * 16, swap)
            block[index, half * 2 : half * 2 + 2] = turned.reshape(2, 8, SUB, 256)

    return make


def unpack(in_ref, lane, swap, rows_ref, row_start):
    def block(index, carry):
        stacked = in_ref[pl.ds(pl.multiple_of(index * 16, 16), 16), :, lane : lane + 256].reshape(256, 256)
        turned = jnp.dot(swap, stacked, preferred_element_type=F32).astype(BF16)
        start = pl.multiple_of(row_start + index * 16, 16)
        for j in range(SUB):
            rows_ref[pl.ds(start, 16), j * 256 : (j + 1) * 256] = turned[j * 16 : (j + 1) * 16, :]
        return carry

    lax.fori_loop(0, 8, block, 0)


def expert_ids(order):
    position = lax.broadcasted_iota(jnp.int32, (128, 32), 0)
    value = {
        order[0]: position // 32,
        order[1]: rem(position // 8, 4),
        order[2]: rem(position // 2, 4),
    }
    return value["z"] * 32 + value["x"] * 8 + value["y"] * 2 + rem(position, 2)


def own_picks(table, pick_ref, early):
    for r in range(3):
        ids = expert_ids(ORDERS[r]).astype(F32)
        named = jnp.zeros((128, 32), F32)
        for k in range(8):
            named = named + (table[k : k + 1, 0:32] == ids).astype(F32)
        before = jnp.dot(named.astype(BF16), early, preferred_element_type=F32)
        keep = (named > 0.5) & (before == float(r))
        pick_ref[r] = keep.astype(F32).astype(BF16)


def scatter_kernel(
    tokens, cotangent, start, table_ref, out_a, out_b, out_c, pick_ref,
    held, tables, first_a, first_b, first_c, second_a, second_b, second_c, rows,
    row_send, row_recv, tab_send, tab_recv, send_two, recv_two, local_two, send_three, recv_three, local_three,
):
    sources, outs = (tokens, cotangent, start), (out_a, out_b, out_c)
    first_hold, second_hold = (first_a, first_b, first_c), (second_a, second_b, second_c)
    place = here()
    plans = [groups_of(order, False) for order in ORDERS]
    entry_barrier(peers_of(place))

    def remote(src, dst, send_sem, recv_sem, target):
        return pltpu.make_async_remote_copy(
            src, dst, send_sem, recv_sem, device_id=device_of(target), device_id_type=MESH
        )

    for step in offsets(("z",))[1:]:
        for u, (one, two, three) in enumerate(plans):
            mine, target, slot = index_of(place, one), moved(place, one, step), slot_id(one, step)
            remote(table_ref, tables.at[u, mine], tab_send.at[u], tab_recv.at[u, slot], target).start()
            remote(sources[u], held.at[u, mine], row_send.at[u], row_recv.at[u, slot], target).start()

    swap = swap_matrix()
    early = lax.broadcasted_iota(jnp.int32, (32, 32), 0) < lax.broadcasted_iota(jnp.int32, (32, 32), 1)
    early = early.astype(F32).astype(BF16)
    position = lax.broadcasted_iota(jnp.int32, (32, 32), 0)

    def origin_of(turn, u):
        step = offsets(plans[u][0])[turn]
        return step, moved(place, plans[u][0], step, -1)

    def build(turn, u, between):
        order = ORDERS[u]
        step, origin = origin_of(turn, u)
        source = place[order[0]] if turn == 0 else origin[order[0]]
        if turn == 0:
            table, block = table_ref, sources[u]
        else:
            table, block = tables.at[u, source], held.at[u, source]
            remote(table, table, tab_send.at[u], tab_recv.at[u, step[0]], origin).wait_recv()
            remote(block, block, row_send.at[u], row_recv.at[u, step[0]], origin).wait_recv()
        value = {order[0]: place[order[0]], order[1]: position // 8, order[2]: rem(position // 2, 4)}
        ids = (value["z"] * 32 + value["x"] * 8 + value["y"] * 2 + rem(position, 2)).astype(F32)
        named = jnp.zeros((32, 32), F32)
        weight = jnp.zeros((32, 32), F32)
        for k in range(8):
            hit = table[k : k + 1, 0:32] == ids
            named = named + hit.astype(F32)
            weight = weight + jnp.where(hit, table[8 + k : 9 + k, 0:32], 0.0)
        before = jnp.dot(named.astype(BF16), early, preferred_element_type=F32)
        keeps = [((named > 0.5) & (before == float(r))).astype(F32) for r in range(3)]
        pick = jnp.concatenate(keeps, axis=0)
        slot_gate = jnp.sum(pick * jnp.concatenate([weight] * 3, axis=0), axis=1, keepdims=True)
        pick = pick.astype(BF16)
        for part in range(4):
            columns = slice(part * 1024, (part + 1) * 1024)
            picked = jnp.dot(pick, block[:, columns], preferred_element_type=F32)
            if u == 1:
                picked = picked * slot_gate
            rows[:, columns] = picked.astype(BF16)
        between()

        def turned(r, carry):
            lanes = pl.ds(pl.multiple_of(r * 256, 256), 256)
            for half in range(2):
                begin = pl.multiple_of(r * 32 + half * 16, 16)
                stacked = jnp.concatenate(
                    [rows[pl.ds(begin, 16), j * 256 : (j + 1) * 256] for j in range(SUB)], axis=0
                )
                tile = jnp.dot(swap, stacked, preferred_element_type=F32).astype(BF16)
                first_hold[u][source, half * 2 : half * 2 + 2, :, :, lanes] = tile.reshape(2, 8, SUB, 256)
            return carry

        lax.fori_loop(0, 3, turned, 0)

    def send(turn, u):
        one, two, three = plans[u]
        source = index_of(origin_of(turn, u)[1], one) if turn else index_of(place, one)
        mine_two = index_of(place, two)
        for hop in offsets(two)[1:]:
            target = moved(place, two, hop)
            remote(
                first_hold[u].at[source, index_of(target, two)],
                second_hold[u].at[mine_two, source],
                send_two.at[u],
                recv_two.at[u, slot_id(two, hop)],
                target,
            ).start()
        pltpu.make_async_copy(
            first_hold[u].at[source, mine_two], second_hold[u].at[mine_two, source], local_two.at[u]
        ).start()

    chunks = [(turn, u) for turn in range(4) for u in range(3)]
    for index, chunk in enumerate(chunks):
        build(*chunk, (lambda: None) if index == 0 else functools.partial(send, *chunks[index - 1]))
    own_picks(table_ref, pick_ref, early)
    send(*chunks[-1])
    for turn in range(4):
        for u, (one, two, three) in enumerate(plans):
            step = offsets(two)[turn]
            mine_two, mine_three = index_of(place, two), index_of(place, three)
            if turn == 0:
                source = mine_two
                block = second_hold[u].at[source]
                pltpu.make_async_copy(block, block, local_two.at[u]).wait()
            else:
                origin = moved(place, two, step, -1)
                source = index_of(origin, two)
                block = second_hold[u].at[source]
                remote(block, block, send_two.at[u], recv_two.at[u, slot_id(two, step)], origin).wait_recv()
            for hop in offsets(three)[1:]:
                target = moved(place, three, hop)
                remote(
                    second_hold[u].at[source, :, index_of(target, three)],
                    outs[u].at[mine_three, source],
                    send_three.at[u],
                    recv_three.at[u],
                    target,
                ).start()
            pltpu.make_async_copy(
                second_hold[u].at[source, :, mine_three], outs[u].at[mine_three, source], local_three.at[u]
            ).start()
    near = moved(place, ("c",), (1,))
    for u, (one, two, three) in enumerate(plans):
        rest = tables.at[u, pl.ds(0, 3)]
        remote(rest, rest, tab_send.at[u], recv_three.at[u], near).wait_send()
        rest = held.at[u, pl.ds(0, 3)]
        remote(rest, rest, row_send.at[u], recv_three.at[u], near).wait_send()
        rest = second_hold[u].at[pl.ds(0, 3)]
        remote(rest, rest, send_two.at[u], recv_three.at[u], near).wait_send()
        rest = outs[u].at[pl.ds(0, 7)]
        bulk = remote(rest, rest, send_three.at[u], recv_three.at[u], near)
        bulk.wait_send()
        bulk.wait_recv()
        mine = outs[u].at[index_of(place, three)]
        pltpu.make_async_copy(mine, mine, local_three.at[u]).wait()


def scatter(routes, gates, tokens, cotangent, start):
    table = jnp.concatenate([routes.T.astype(F32), gates.T], axis=0)
    table = jnp.pad(table, ((0, 0), (0, 96)))
    results = pl.pallas_call(
        scatter_kernel,
        out_shape=[jax.ShapeDtypeStruct((8, 4, 4, SUB, 768), BF16)] * 3
        + [jax.ShapeDtypeStruct((3, 128, 32), BF16)],
        in_specs=[VM] * 4,
        out_specs=[ANY] * 3 + [VM],
        scratch_shapes=[pltpu.VMEM((3, 4, 32, 4096), BF16), pltpu.VMEM((3, 4, 16, 128), F32)]
        + [pltpu.VMEM((4, 4, 8, SUB, 768), BF16)] * 6
        + [pltpu.VMEM((96, 4096), BF16)]
        + [pltpu.SemaphoreType.DMA((3,)), pltpu.SemaphoreType.DMA((3, 4))] * 2
        + [pltpu.SemaphoreType.DMA((3,)), pltpu.SemaphoreType.DMA((3, 8))]
        + [pltpu.SemaphoreType.DMA((3,))] * 4,
        name="scatter",
        compiler_params=pltpu.CompilerParams(
            collective_id=0, has_side_effects=True, vmem_limit_bytes=48 << 20
        ),
    )(tokens, cotangent, start, table)
    return [result.reshape(128, SUB, 768) for result in results[:3]], results[3]


def unpack_unit(in_ref, u, r, swap, rows_ref):
    order, home = ORDERS[r], ORDERS[u]

    def block(index, carry):
        pieces = []
        for spot in range(16):
            value = {order[2]: index // 2, order[1]: spot // 4, order[0]: spot % 4}
            third = value[home[2]] * 2 + rem(index, 2)
            pieces.append(in_ref[third * 16 + value[home[1]] * 4 + value[home[0]], :, r * 256 : (r + 1) * 256])
        stacked = jnp.concatenate(pieces, axis=0)
        turned = jnp.dot(swap, stacked, preferred_element_type=F32).astype(BF16)
        start = pl.multiple_of(r * 128 + index * 16, 16)
        for j in range(SUB):
            rows_ref[pl.ds(start, 16), j * 256 : (j + 1) * 256] = turned[j * 16 : (j + 1) * 16, :]
        return carry

    lax.fori_loop(0, 8, block, 0)


CONTRACT_LAST = (((1,), (1,)), ((), ()))


def last_dot(left, right):
    return lax.dot_general(left, right, CONTRACT_LAST, preferred_element_type=F32)


def results_out(out_gate, out_up, gate_w, up_w, rows):
    def tile(index, carry):
        start = pl.multiple_of(index * 256, 256)
        summed = last_dot(out_gate[...], gate_w[pl.ds(start, 256), :])
        summed = summed + last_dot(out_up[...], up_w[pl.ds(start, 256), :])
        rows[:, pl.ds(start, 256)] = summed.astype(BF16)
        return carry

    lax.fori_loop(0, 16, tile, 0)


def first_expert_kernel(
    in_a, in_b, in_c, gate_h, up_h, down_h, out_a, out_b, out_c, one_ref, two_ref, ag_ref, au_ref,
    gate_w, up_w, down_w, x_rows, c_rows, v_rows, out_gate, out_up, sems, *net,
):
    place = here()
    greet(peers_of(place))
    copies = [
        pltpu.make_async_copy(src, dst, sems.at[i])
        for i, (src, dst) in enumerate(((gate_h, gate_w), (up_h, up_w), (down_h, down_w)))
    ]
    for copy in copies:
        copy.start()
    swap = swap_matrix()
    for u, (source, rows) in enumerate(((in_a, x_rows), (in_b, c_rows), (in_c, v_rows))):
        for r in range(3):
            unpack_unit(source, u, r, swap, rows)
    for copy in copies:
        copy.wait()

    def tile(index, carry):
        columns = pl.ds(pl.multiple_of(index * 256, 256), 256)
        gate_t, up_t = gate_w[:, columns], up_w[:, columns]
        pre_gate = jnp.dot(x_rows[...], gate_t, preferred_element_type=F32)
        pre_up = jnp.dot(x_rows[...], up_t, preferred_element_type=F32)
        back_grad = last_dot(c_rows[...], down_w[columns, :])
        logistic = 1.0 / (1.0 + jnp.exp(-pre_gate))
        slope_one = logistic * (1.0 + pre_gate * (1.0 - logistic))
        slope_two = logistic * (1.0 - logistic) * (2.0 + pre_gate * (1.0 - 2.0 * logistic))
        scale_one = back_grad * slope_one
        scale_two = back_grad * pre_up * slope_two
        one_ref[:, columns] = scale_one
        two_ref[:, columns] = scale_two
        along_gate = jnp.dot(v_rows[...], gate_t, preferred_element_type=F32)
        along_up = jnp.dot(v_rows[...], up_t, preferred_element_type=F32)
        ag_ref[:, columns] = along_gate
        au_ref[:, columns] = along_up
        out_gate[:, columns] = (scale_one * along_up + scale_two * along_gate).astype(BF16)
        out_up[:, columns] = (scale_one * along_gate).astype(BF16)
        return carry

    lax.fori_loop(0, 3, tile, 0)
    results_out(out_gate, out_up, gate_w, up_w, x_rows)
    await_greetings(peers_of(place))
    exchange_steps(place, True, maker(True, x_rows, swap), (out_a, out_b, out_c), net)


def first_expert(blocks, gate_w, up_w, down_w):
    hidden = jax.ShapeDtypeStruct((384, 768), F32)
    results = pl.pallas_call(
        first_expert_kernel,
        out_shape=arriving(True) + [hidden] * 4,
        in_specs=[VM] * 3 + [ANY] * 3,
        out_specs=[ANY] * 3 + [VM] * 4,
        scratch_shapes=[pltpu.VMEM((4096, 768), BF16)] * 2
        + [pltpu.VMEM((768, 4096), BF16)]
        + [pltpu.VMEM((384, 4096), BF16)] * 3
        + [pltpu.VMEM((384, 768), BF16)] * 2
        + [pltpu.SemaphoreType.DMA((3,))]
        + net_scratch(True),
        name="first_expert",
        compiler_params=pltpu.CompilerParams(
            collective_id=1, has_side_effects=True, vmem_limit_bytes=62 << 20
        ),
    )(*blocks, gate_w, up_w, down_w)
    return as_messages(results[:3]), results[3:]


def first_scalars(total, entries):
    square = total[0:1, 0:1] / entries
    cross = total[1:2, 0:1] / entries
    image = total[2:3, 0:1] / entries
    norm_square = square + EPSILON
    norm = jnp.sqrt(norm_square)
    alpha = cross / norm_square
    variance = (image - 2.0 * alpha * cross + alpha * alpha * square) / norm_square
    beta = jnp.sqrt(jnp.maximum(variance, 0.0) + EPSILON)
    return {"norm": norm, "alpha": alpha, "beta": beta, "square": square}


def second_expert_kernel(
    entries, in_a, in_b, in_c, total, one_ref, two_ref, ag_ref, au_ref, gate_h, up_h, out_a, out_b, out_c,
    gate_w, up_w, v_rows, out_gate, out_up, sems, *net,
):
    place = here()
    greet(peers_of(place))
    copies = [
        pltpu.make_async_copy(src, dst, sems.at[i])
        for i, (src, dst) in enumerate(((gate_h, gate_w), (up_h, up_w)))
    ]
    for copy in copies:
        copy.start()
    swap = swap_matrix()
    for r, source in enumerate((in_a, in_b, in_c)):
        unpack(source, 0, swap, v_rows, r * 128)
    scalars = first_scalars(total[...], entries)
    scale = 1.0 / (scalars["norm"] * scalars["beta"])
    shift = scalars["alpha"] * scale
    for copy in copies:
        copy.wait()

    def tile(index, carry):
        columns = pl.ds(pl.multiple_of(index * 256, 256), 256)
        along_gate = jnp.dot(v_rows[...], gate_w[:, columns], preferred_element_type=F32)
        along_up = jnp.dot(v_rows[...], up_w[:, columns], preferred_element_type=F32)
        along_gate = along_gate * scale - ag_ref[:, columns] * shift
        along_up = along_up * scale - au_ref[:, columns] * shift
        scale_one = one_ref[:, columns]
        out_gate[:, columns] = (scale_one * along_up + two_ref[:, columns] * along_gate).astype(BF16)
        out_up[:, columns] = (scale_one * along_gate).astype(BF16)
        return carry

    lax.fori_loop(0, 3, tile, 0)
    results_out(out_gate, out_up, gate_w, up_w, v_rows)
    await_greetings(peers_of(place))
    exchange_steps(place, True, maker(True, v_rows, swap), (out_a, out_b, out_c), net)


def second_expert(entries, blocks, total, hidden, gate_w, up_w):
    results = pl.pallas_call(
        functools.partial(second_expert_kernel, entries),
        out_shape=arriving(True),
        in_specs=[VM] * 8 + [ANY] * 2,
        out_specs=[ANY] * 3,
        scratch_shapes=[pltpu.VMEM((4096, 768), BF16)] * 2
        + [pltpu.VMEM((384, 4096), BF16)]
        + [pltpu.VMEM((384, 768), BF16)] * 2
        + [pltpu.SemaphoreType.DMA((2,))]
        + net_scratch(True),
        name="second_expert",
        compiler_params=pltpu.CompilerParams(
            collective_id=3, has_side_effects=True, vmem_limit_bytes=56 << 20
        ),
    )(*blocks, total, *hidden, gate_w, up_w)
    return as_messages(results)


CONTRACT_FIRST = (((0,), (0,)), ((), ()))


def gather_image(blocks, pick_ref, swap, rows, image):
    for r in range(3):
        unpack(blocks[r], 0, swap, rows, r * 128)
    picks = jnp.concatenate([pick_ref[r] for r in range(3)], axis=0)
    for part in range(8):
        columns = slice(part * 512, (part + 1) * 512)
        image[:, columns] = lax.dot_general(picks, rows[:, columns], CONTRACT_FIRST, preferred_element_type=F32)


def as_tile(values):
    row = lax.broadcasted_iota(jnp.int32, (8, 128), 0)
    tile = jnp.zeros((8, 128), F32)
    for index, value in enumerate(values):
        tile = jnp.where(row == index, value, tile)
    return tile


def whole_sum(array):
    return jnp.sum(jnp.sum(array, axis=0, keepdims=True), axis=1, keepdims=True)


def turn_kernel(
    in_a, in_b, in_c, pick_ref, start, image, out_a, out_b, out_c, total_ref, rows, tile_a, tile_b, tile_c,
    sum_send, sum_recv, *net,
):
    place = here()
    greet(peers_of(place))
    swap = swap_matrix()
    gather_image((in_a, in_b, in_c), pick_ref, swap, rows, image)
    anchor = start[...].astype(F32)
    found = image[...]
    part = as_tile([whole_sum(anchor * anchor), whole_sum(anchor * found), whole_sum(found * found)])
    for quarter in range(4):
        columns = slice(quarter * 1024, (quarter + 1) * 1024)
        narrow = image[:, columns].astype(BF16)
        for r in range(3):
            picked = jnp.dot(pick_ref[r], narrow, preferred_element_type=F32)
            rows[r * 128 : (r + 1) * 128, columns] = picked.astype(BF16)
    await_greetings(peers_of(place))
    reduction = Reduction(place, (tile_a, tile_b, tile_c), sum_send, sum_recv)
    total_ref[...] = exchange_steps(
        place, False, maker(False, rows, swap), (out_a, out_b, out_c), net, reduction, part
    )


def turn(blocks, pick, start):
    results = pl.pallas_call(
        turn_kernel,
        out_shape=[jax.ShapeDtypeStruct(start.shape, F32)]
        + arriving(False)
        + [jax.ShapeDtypeStruct((8, 128), F32)],
        in_specs=[VM] * 5,
        out_specs=[VM] + [ANY] * 3 + [VM],
        scratch_shapes=[pltpu.VMEM((384, 4096), BF16)] + reduction_scratch() + net_scratch(False),
        name="turn",
        compiler_params=pltpu.CompilerParams(
            collective_id=2, has_side_effects=True, vmem_limit_bytes=40 << 20
        ),
    )(*blocks, pick, start)
    return results[0], as_messages(results[1:4]), results[4]


def finish_kernel(
    entries, in_a, in_b, in_c, pick_ref, start, first_image, total_ref, basis_ref, residual_ref, tri_ref,
    rows, image, tile_a, tile_b, tile_c, sum_send, sum_recv,
):
    place = here()
    reduction = Reduction(place, (tile_a, tile_b, tile_c), sum_send, sum_recv)
    peers = []
    for axes in REDUCE_GROUPS:
        peers += [moved(place, axes, step) for step in offsets(axes)[1:]]
    entry_barrier(peers)
    swap = swap_matrix()
    gather_image((in_a, in_b, in_c), pick_ref, swap, rows, image)
    scalars = first_scalars(total_ref[...], entries)
    norm, alpha, beta = scalars["norm"], scalars["alpha"], scalars["beta"]
    base = start[...].astype(F32) / norm
    basis = ((first_image[...] / norm - alpha * base) / beta).astype(BF16)
    basis_ref[...] = basis
    wide = basis.astype(F32)
    found = image[...]
    partial = as_tile(
        [
            whole_sum(wide * found),
            whole_sum(found * found),
            whole_sum(base * found),
            whole_sum(wide * wide),
            whole_sum(wide * base),
            whole_sum(base * base),
        ]
    )
    reduction.send(0, partial)
    reduction.send(1, reduction.receive(0))
    reduction.send(2, reduction.receive(1))
    total = reduction.receive(2) / entries
    alpha_one = total[0:1, 0:1]
    square = (
        total[1:2, 0:1]
        - 2.0 * alpha_one * total[0:1, 0:1]
        - 2.0 * beta * total[2:3, 0:1]
        + alpha_one * alpha_one * total[3:4, 0:1]
        + 2.0 * alpha_one * beta * total[4:5, 0:1]
        + beta * beta * total[5:6, 0:1]
    )
    beta_two = jnp.sqrt(jnp.maximum(square, 0.0) + EPSILON)
    residual_ref[...] = image[...] - alpha_one * basis_ref[...].astype(F32) - beta * (start[...].astype(F32) / norm)
    tri_ref[...] = as_tile([alpha, beta, alpha_one, beta_two])


def finish(entries, blocks, pick, start, first_image, total):
    return pl.pallas_call(
        functools.partial(finish_kernel, entries),
        out_shape=[
            jax.ShapeDtypeStruct(start.shape, BF16),
            jax.ShapeDtypeStruct(start.shape, F32),
            jax.ShapeDtypeStruct((8, 128), F32),
        ],
        in_specs=[VM] * 7,
        out_specs=[VM] * 3,
        scratch_shapes=[pltpu.VMEM((384, 4096), BF16), pltpu.VMEM(start.shape, F32)] + reduction_scratch(),
        name="finish",
        compiler_params=pltpu.CompilerParams(
            collective_id=5, has_side_effects=True, vmem_limit_bytes=32 << 20
        ),
    )(*blocks, pick, start, first_image, total)


def on_device(tokens, cotangent, start, gates, routes, w_gate, w_up, w_down):
    entries = float(128 * tokens.shape[0] * tokens.shape[1])
    gate_w, up_w, down_w = w_gate[0], w_up[0], w_down[0]
    arrived, pick = scatter(routes, gates, tokens, cotangent, start)
    returned, hidden = first_expert(arrived, gate_w, up_w, down_w)
    image_zero, arrived, total = turn(returned, pick, start)
    returned = second_expert(entries, arrived, total, hidden, gate_w, up_w)
    basis, residual, tri = finish(entries, returned, pick, start, image_zero, total)
    return basis, residual, tri[:4, 0]


def solution(mesh):
    rows = P(("dp", "expert"), None)
    experts = P(("dp", "expert"), None, None)
    return jax.shard_map(
        on_device,
        mesh=mesh,
        in_specs=(rows,) * 5 + (experts,) * 3,
        out_specs=(rows, rows, P()),
        check_vma=False,
    )
```
